512 devices in a mesh: ka: 64 (over z, y_hi, core), ga: 8 (over y_lo, x).
Axes of the slice: x: 4, y: 4 (y_hi: 2, y_lo: 2; y = y_hi * 2 + y_lo), z: 16, core: 2. Of those that a mesh axis runs over, the one named last changes fastest.
Arguments:
- orbitals: bfloat16 [64, 16, 4096], P('ka', None, 'ga'), may hold values from -6 to 6
- interp_vectors: bfloat16 [4096, 4096], P(None, 'ga'), may hold values from -0.09375 to 0.09375
- screening: bfloat16 [9216, 4096], P('ka', 'ga'), may hold values from 0.049804688 to 2
- bare_coulomb: float32 [4096], P('ga'), may hold values from 0.05 to 2
- slab_kpoints: int32 [64], P('ka'), may hold values from 0 to 9215, as said below
Outputs:
- kernel: float32 [64, 7, 1, 4096], P('ka', None, None, 'ga')
The draws below stay inside these ranges and needn't reach their ends.
Inputs may be any that keep to these rules, and one draw needn't show every extreme that they name: `slab_kpoints`: distinct grid points, each written as ix * 96 + iy with ix and iy its two grid coordinates.
All inputs are finite; a program needn't handle non-finite values.
Results may differ from the reference program's by a relative error of at most 0.0049.
Values may be sent and summed in bfloat16 or wider, within the bound.
No kernel may reach another device: no remote copies, remote signals or barrier semaphores. Data moves between devices by JAX's collectives and lax.ppermute only.
A program may use at most 64 MiB of HBM per device.

```python
import math
import jax
import jax.numpy as jnp

NV = 8
NC = 8
NG = 4096
NPTS = 4096
NKX = 96
KD = 1
RSTEPS = 3
NK = 9216
NOFF = 7
SLAB = 64
N_KA = 64


def draw_slab_kpoints(key, part):
    return jax.random.permutation(key, NK)[:SLAB].astype(jnp.int32)


def block_scale(stream_key, shape, cuts, least, largest):
    level = 1.0
    for dim, parts in cuts:
        draws = jax.random.uniform(jax.random.fold_in(jax.random.fold_in(stream_key, 6), dim), (parts,), jnp.float32, least / len(cuts), largest / len(cuts))
        level = level * jnp.repeat(jnp.exp(draws), shape[dim] // parts).reshape((-1,) + (1,) * (len(shape) - 1 - dim))
    return level


def gaussian(stream_key, extent, scale, reach, cuts=(), kind=jnp.bfloat16):
    gain = block_scale(stream_key, extent, cuts, -0.22, 0.18) if cuts else 1.0
    values = jax.random.normal(stream_key, extent, jnp.float32) * scale * gain
    return jnp.minimum(jnp.maximum(values, -reach), reach).astype(kind)


def setup_inputs(seed: int = 0) -> dict:
    key_list = jax.random.split(jax.random.key(seed), 6)
    orbitals = gaussian(key_list[0], (SLAB, NV + NC, NPTS), 1.0, 6.0, ((0, 64), (2, 8)))
    interp_vectors = gaussian(key_list[1], (NPTS, NG), NPTS ** -0.5, 0.09375, ((1, 8),))
    screening = jnp.clip(jnp.exp(math.log(2.0) - 3.6927934 * jax.random.uniform(key_list[2], (NK, NG), jnp.float32) ** block_scale(key_list[2], (NK, NG), ((0, 64), (1, 8)), -0.2, 0.2)), 0.049804688, 2.0).astype(jnp.bfloat16)
    bare_coulomb = jnp.clip(jnp.exp(math.log(2.0) - 3.6888794 * jax.random.uniform(key_list[3], (NG,), jnp.float32) ** block_scale(key_list[3], (NG,), ((0, 8),), -0.2, 0.2)), 0.05, 2.0)
    slab_kpoints = draw_slab_kpoints(jax.random.fold_in(key_list[5], 71), 0)
    return dict(orbitals=orbitals, interp_vectors=interp_vectors, screening=screening, bare_coulomb=bare_coulomb, slab_kpoints=slab_kpoints)


def band_products(first_set, second_set):
    product = first_set.astype(jnp.float32)[:, :, None, :, None, :] * second_set.astype(jnp.float32)[:, None, :, None, :, :]
    dims_in = product.shape
    return product.reshape(dims_in[0], dims_in[1], dims_in[2], dims_in[3] * dims_in[4], dims_in[5]).astype(jnp.bfloat16)


def project(points, interp_vectors):
    dims_in = points.shape
    flattened = points.reshape(-1, dims_in[-1])
    pair_waves = jnp.dot(flattened, interp_vectors, preferred_element_type=jnp.float32)
    return pair_waves.astype(jnp.bfloat16).reshape(dims_in[:-1] + (interp_vectors.shape[1],))


def momentum_index(first_point, second_point):
    row_step = (first_point // NKX - second_point // NKX) % NKX
    col_step = (first_point % NKX - second_point % NKX) % NKX
    return (row_step * NKX + col_step).astype(jnp.int32)


def reference(orbitals, interp_vectors, screening, bare_coulomb, slab_kpoints):
    blocks = orbitals.reshape(N_KA, KD, NV + NC, NPTS)
    valence = blocks[:, :, :NV]
    conduct = blocks[:, :, NV:]
    own_product = valence.astype(jnp.float32)[:, :, :, None, :] * conduct.astype(jnp.float32)[:, :, None, :, :]
    exchange_points = own_product.reshape(N_KA, KD, NV * NC, NPTS).astype(jnp.bfloat16)
    exchange_waves = project(exchange_points, interp_vectors)
    weighted_x = (exchange_waves.astype(jnp.float32) * bare_coulomb).astype(jnp.bfloat16)
    grid_points = slab_kpoints.reshape(N_KA, KD)
    pieces = []
    for offset in range(-RSTEPS, RSTEPS + 1):
        partner = jnp.roll(blocks, offset, axis=0)
        partner_ex = jnp.roll(exchange_waves, offset, axis=0)
        partner_k = jnp.roll(grid_points, offset, axis=0)
        cond_pairs = band_products(conduct, partner[:, :, NV:])
        vale_pairs = band_products(valence, partner[:, :, :NV])
        pair_waves = project(jnp.concatenate([cond_pairs, vale_pairs], axis=3), interp_vectors)
        momentum = momentum_index(grid_points[:, :, None], partner_k[:, None, :])
        screen_rows = screening[momentum].astype(jnp.float32)
        weighted = (pair_waves[:, :, :, :NC * NC].astype(jnp.float32) * screen_rows[:, :, :, None, :]).astype(jnp.bfloat16)
        direct = jnp.einsum('bklxg,bklyg->bklxy', weighted.astype(jnp.float32), pair_waves[:, :, :, NC * NC:].astype(jnp.float32))
        direct = direct.reshape(N_KA, KD, KD, NC, NC, NV, NV).transpose(0, 1, 2, 5, 3, 6, 4).reshape(N_KA, KD, KD, -1)
        exch_term = jnp.einsum('bkxg,blyg->bklxy', weighted_x.astype(jnp.float32), partner_ex.astype(jnp.float32))
        exch_term = exch_term.reshape(N_KA, KD, KD, -1)
        pieces.append(2.0 * exch_term - direct)
    kernel = jnp.stack(pieces, axis=2).reshape(SLAB, NOFF, KD, (NV * NC) ** 2)
    return kernel * (NG ** -0.5)
```

```python
import jax
import jax.numpy as jnp
from jax import lax
from jax.sharding import PartitionSpec as P

NV = 8
NC = 8
NG = 4096
NKX = 96
RSTEPS = 3
NEAR = 8


def near_groups(size, shift):
    return [
        [(start + shift + j) % size for j in range(NEAR)] for start in range(0, size, NEAR)
    ]


def far_groups(size):
    return [[j + start for start in range(0, size, NEAR)] for j in range(NEAR)]


def copy_for_each(shard, axis, size, groups=None):
    return lax.all_to_all(
        jnp.broadcast_to(shard[None], (size, *shard.shape)),
        axis,
        0,
        0,
        tiled=True,
        axis_index_groups=groups,
    )


def momentum_index(first_point, second_point):
    row_step = first_point // NKX - second_point // NKX
    col_step = first_point % NKX - second_point % NKX
    row_step = jnp.where(row_step < 0, row_step + NKX, row_step)
    col_step = jnp.where(col_step < 0, col_step + NKX, col_step)
    return row_step * NKX + col_step


def window(orbitals, size):
    place = lax.axis_index("ka") % NEAR
    block = copy_for_each(orbitals, "ka", NEAR, near_groups(size, 0))
    shifted = copy_for_each(orbitals, "ka", NEAR, near_groups(size, NEAR // 2))
    half = NEAR // 2
    low = jnp.concatenate([shifted[:half], block])
    high = jnp.concatenate([block, shifted[half:]])
    twelve = jnp.where(place < half, low, high)
    start = jnp.where(place < half, place + half - RSTEPS, place - RSTEPS)
    return lax.dynamic_slice_in_dim(twelve, start, 2 * RSTEPS + 1, 0)


def asked_rows(points, screening, size):
    offsets = range(-RSTEPS, RSTEPS + 1)
    partners = jnp.stack([jnp.roll(points, d) for d in offsets], axis=0)
    wanted = momentum_index(points[None, :], partners)
    table_rows = screening.shape[0]
    local = wanted - lax.axis_index("ka") * table_rows
    blocks = size // NEAR
    local = local.reshape(-1, blocks, NEAR).transpose(2, 1, 0)
    picker = (local[..., None] == jnp.arange(table_rows, dtype=jnp.int32)).astype(jnp.bfloat16)
    replies = jnp.dot(
        picker.reshape(-1, table_rows), screening, preferred_element_type=jnp.float32
    ).astype(jnp.bfloat16)
    replies = replies.reshape(NEAR, blocks * local.shape[-1], -1)
    near = lax.all_to_all(
        replies, "ka", 0, 0, tiled=True, axis_index_groups=near_groups(size, 0)
    )
    near = near.astype(jnp.float32).sum(axis=0).astype(jnp.bfloat16)
    near = near.reshape(blocks, local.shape[-1], -1)
    far = lax.all_to_all(near, "ka", 0, 0, tiled=True, axis_index_groups=far_groups(size))
    return far.astype(jnp.float32).sum(axis=0)


def band_products(first, second):
    product = first.astype(jnp.float32)[:, :, None, :] * second.astype(jnp.float32)[:, None, :, :]
    return product.reshape(product.shape[0], -1, product.shape[-1]).astype(jnp.bfloat16)


def per_device(orbitals, interp_vectors, screening, bare_coulomb, slab_kpoints):
    size = lax.axis_size("ka")
    parts = lax.axis_size("ga")
    points = copy_for_each(slab_kpoints, "ka", size).reshape(-1)
    near = window(orbitals[0], size)
    count = near.shape[0]
    full = copy_for_each(near, "ga", parts)
    full = jnp.moveaxis(full, 0, 2).reshape(count, NV + NC, -1)
    own = jnp.broadcast_to(full[RSTEPS][None], full.shape)
    screen_rows = asked_rows(points, screening, size)
    rows = jnp.concatenate(
        [
            band_products(own[:, NV:], full[:, NV:]),
            band_products(own[:, :NV], full[:, :NV]),
            band_products(full[:, :NV], full[:, NV:]),
        ],
        axis=1,
    )
    total = rows.shape[1]
    waves = jnp.dot(
        rows.reshape(count * total, -1), interp_vectors, preferred_element_type=jnp.float32
    ).astype(jnp.bfloat16).reshape(count, total, -1)
    waves = waves[::-1]
    exchange = waves[:, NC * NC + NV * NV :]
    weighted_x = (exchange[RSTEPS].astype(jnp.float32) * bare_coulomb).astype(jnp.bfloat16)
    exch = jnp.einsum("xg,dyg->dxy", weighted_x, exchange, preferred_element_type=jnp.float32)
    weighted = (waves[:, : NC * NC].astype(jnp.float32) * screen_rows[:, None, :]).astype(
        jnp.bfloat16
    )
    direct = jnp.einsum(
        "dxg,dyg->dxy",
        weighted,
        waves[:, NC * NC : NC * NC + NV * NV],
        preferred_element_type=jnp.float32,
    )
    direct = direct.reshape(count, NC, NC, NV, NV).transpose(3, 0, 1, 4, 2)
    exch = exch.reshape(count, NV, NC, NV * NC).transpose(1, 0, 2, 3)
    partial = 2.0 * exch.reshape(NV, count, -1) - direct.reshape(NV, count, -1)
    arrived = lax.all_to_all(partial, "ga", 0, 0, tiled=True)
    return (arrived.sum(axis=0) * NG ** (-0.5))[None, :, None, :]


def solution(mesh):
    in_specs = (P("ka", None, "ga"), P(None, "ga"), P("ka", "ga"), P("ga"), P("ka"))
    out_specs = P("ka", None, None, "ga")
    return jax.shard_map(
        per_device, mesh=mesh, in_specs=in_specs, out_specs=out_specs, check_vma=False
    )
```

```python
import jax
import jax.numpy as jnp
from jax import lax
from jax.experimental import pallas as pl
from jax.experimental.pallas import tpu as pltpu
from jax.sharding import PartitionSpec as P


NV = 8
NC = 8
NG = 4096
NKX = 96
RSTEPS = 3
NOFF = 2 * RSTEPS + 1
NEAR = 8
LANES = 128
BANDS = NV + NC
PAIRS = NC * NC


def near_groups(size):
    return [[start + j for j in range(NEAR)] for start in range(0, size, NEAR)]


def far_groups(size):
    return [[j + start for start in range(0, size, NEAR)] for j in range(NEAR)]


def swap(tiles, axis, groups=None):
    return lax.all_to_all(tiles, axis, 0, 0, tiled=True, axis_index_groups=groups)


VMEM = pl.BlockSpec(memory_space=pltpu.VMEM)
SMEM = pl.BlockSpec(memory_space=pltpu.SMEM)


def message_kernel(point_ref, own_ref, out_ref):
    chunk = own_ref.shape[1]
    row = point_ref[0] // NKX
    col = point_ref[0] - row * NKX
    lane = lax.broadcasted_iota(jnp.int32, (NEAR, chunk), 1)
    coords = jnp.where(lane < LANES, row, col).astype(jnp.float32).astype(jnp.bfloat16)
    for j in range(out_ref.shape[0]):
        out_ref[j, :BANDS, :] = own_ref[...]
        out_ref[j, BANDS:, :] = coords


def message_of(points, own):
    return pl.pallas_call(
        message_kernel,
        out_shape=jax.ShapeDtypeStruct((NEAR, BANDS + NEAR, own.shape[1]), own.dtype),
        in_specs=[SMEM, VMEM],
        out_specs=VMEM,
        compiler_params=pltpu.CompilerParams(vmem_limit_bytes=2 << 20),
        name="message",
    )(points, own)


def edges_kernel(place_ref, block_ref, coords_ref, edge_ref):
    rows = [block_ref[j, BANDS : BANDS + 1, : 2 * LANES] for j in range(NEAR)]
    rows = jnp.concatenate([r.astype(jnp.float32) for r in rows], axis=0)
    for b in range(coords_ref.shape[0]):
        coords_ref[b] = rows.astype(jnp.bfloat16)
    inner = lax.rem(place_ref[0], NEAR)
    first = jnp.where(inner < NEAR // 2, 0, NEAR - RSTEPS)
    for n in range(RSTEPS):
        edge_ref[n * BANDS : (n + 1) * BANDS, :] = block_ref[first + n, :BANDS, :]


def edges_of(place, block, blocks):
    return pl.pallas_call(
        edges_kernel,
        out_shape=(
            jax.ShapeDtypeStruct((blocks, NEAR, 2 * LANES), block.dtype),
            jax.ShapeDtypeStruct((RSTEPS * BANDS, block.shape[2]), block.dtype),
        ),
        in_specs=[SMEM, VMEM],
        out_specs=(VMEM, VMEM),
        compiler_params=pltpu.CompilerParams(vmem_limit_bytes=2 << 20),
        name="edges",
    )(place, block)


def edge_route(size):
    route = []
    for k in range(size):
        start, inner = k - k % NEAR, k % NEAR
        if inner < RSTEPS:
            route.append((k, (start - NEAR + NEAR - 1 - inner) % size))
        elif inner >= NEAR - RSTEPS:
            route.append((k, (start + NEAR + NEAR - 1 - inner) % size))
    return route


def window_kernel(place_ref, block_ref, edge_ref, out_ref):
    inner = lax.rem(place_ref[0], NEAR)
    copies = out_ref.shape[0]

    def put(n, value):
        for g in range(copies):
            out_ref[g, n * BANDS : (n + 1) * BANDS, :] = value

    for n in range(NOFF):
        at = inner + (n - RSTEPS)
        inside = jnp.logical_and(at >= 0, at < NEAR)
        over = jnp.where(at < 0, at + RSTEPS, at - NEAR)

        @pl.when(inside)
        def _():
            put(n, block_ref[at, :BANDS, :])

        @pl.when(jnp.logical_not(inside))
        def _():
            rows = pl.ds(pl.multiple_of(over * BANDS, BANDS), BANDS)
            put(n, edge_ref[rows, :])


def window_of(place, block, edge, copies):
    return pl.pallas_call(
        window_kernel,
        out_shape=jax.ShapeDtypeStruct((copies, NOFF * BANDS, block.shape[2]), block.dtype),
        in_specs=[SMEM, VMEM, VMEM],
        out_specs=VMEM,
        compiler_params=pltpu.CompilerParams(vmem_limit_bytes=4 << 20),
        name="window",
    )(place, block, edge)


def near_sum_kernel(rows_ref, out_ref):
    total = rows_ref[0].astype(jnp.float32)
    for b in range(1, rows_ref.shape[0]):
        total = total + rows_ref[b].astype(jnp.float32)
    for b in range(out_ref.shape[0]):
        out_ref[b] = total[b * NOFF : (b + 1) * NOFF].astype(out_ref.dtype)


def near_sum(rows, blocks):
    return pl.pallas_call(
        near_sum_kernel,
        out_shape=jax.ShapeDtypeStruct((blocks, NOFF, rows.shape[2]), rows.dtype),
        in_specs=[VMEM],
        out_specs=VMEM,
        compiler_params=pltpu.CompilerParams(vmem_limit_bytes=4 << 20),
        name="near_sum",
    )(rows)


def result_kernel(terms_ref, out_ref):
    total = terms_ref[0]
    for g in range(1, terms_ref.shape[0]):
        total = total + terms_ref[g]
    out_ref[...] = total * NG ** (-0.5)


def result_of(terms):
    return pl.pallas_call(
        result_kernel,
        out_shape=jax.ShapeDtypeStruct(terms.shape[1:], terms.dtype),
        in_specs=[VMEM],
        out_specs=VMEM,
        compiler_params=pltpu.CompilerParams(vmem_limit_bytes=2 << 20),
        name="result",
    )(terms)


def pick_kernel(place_ref, grid_ref, table_ref, out_ref, local_ref, hot_ref):
    size = grid_ref.shape[0]
    blocks = size // NEAR
    table_rows = table_ref.shape[0]
    row = grid_ref[:, :LANES].astype(jnp.float32)
    col = grid_ref[:, LANES:].astype(jnp.float32)
    base = (place_ref[0] * table_rows).astype(jnp.float32)
    for i in range(NOFF):
        d = i - RSTEPS
        row_step = row - jnp.roll(row, d, axis=0) if d else jnp.zeros_like(row)
        col_step = col - jnp.roll(col, d, axis=0) if d else jnp.zeros_like(col)
        row_step = jnp.where(row_step < 0, row_step + NKX, row_step)
        col_step = jnp.where(col_step < 0, col_step + NKX, col_step)
        local_ref[i * size : (i + 1) * size, :] = row_step * NKX + col_step - base
    lane = lax.broadcasted_iota(jnp.int32, (blocks, LANES), 1).astype(jnp.float32)
    for j in range(NEAR):
        for i in range(NOFF):
            local = local_ref[pl.ds(i * size + j, blocks, stride=NEAR), :]
            rows = pl.ds(j * blocks * NOFF + i, blocks, stride=NOFF)
            for part in range(hot_ref.shape[0]):
                hot_ref[part, rows, :] = jnp.where(local == lane + part * LANES, 1.0, 0.0)
    total = None
    for part in range(hot_ref.shape[0]):
        count = min(LANES, table_rows - part * LANES)
        term = jnp.dot(
            hot_ref[part, :, :count].astype(jnp.bfloat16),
            table_ref[part * LANES : part * LANES + count, :],
            preferred_element_type=jnp.float32,
        )
        total = term if total is None else total + term
    out_ref[...] = total.astype(jnp.bfloat16)


def pick_rows(place, grid, table):
    size = grid.shape[0]
    return pl.pallas_call(
        pick_kernel,
        out_shape=jax.ShapeDtypeStruct((size * NOFF, table.shape[1]), jnp.bfloat16),
        in_specs=[SMEM, VMEM, VMEM],
        out_specs=VMEM,
        scratch_shapes=[
            pltpu.VMEM((NOFF * size, LANES), jnp.float32),
            pltpu.VMEM((pl.cdiv(table.shape[0], LANES), size * NOFF, LANES), jnp.float32),
        ],
        compiler_params=pltpu.CompilerParams(vmem_limit_bytes=6 << 20),
        name="pick_rows",
    )(place, grid, table)


def outer_rows(singles, many):
    rows = []
    for h in range(0, singles.shape[0], 2):
        both = jnp.concatenate(
            [singles[h : h + 1] * many, singles[h + 1 : h + 2] * many], axis=0
        )
        rows.append(both.astype(jnp.bfloat16))
    return rows


def waves_kernel(
    full_ref, vec_ref, bare_ref, cond_ref, vale_ref, exch_ref, perm_ref, pts_ref, acc_ref
):
    parts = full_ref.shape[0]
    chunk = full_ref.shape[2]
    step = 3 * PAIRS

    def put(start, pieces):
        for h, piece in enumerate(pieces):
            pts_ref[start + 2 * NV * h : start + 2 * NV * (h + 1), :] = piece

    def add_chunk(s, carry):
        own = full_ref[s, RSTEPS * BANDS : (RSTEPS + 1) * BANDS, :].astype(jnp.float32)
        own_v, own_c = own[:NV], own[NV:]
        for n in range(NOFF):
            there = full_ref[s, n * BANDS : (n + 1) * BANDS, :].astype(jnp.float32)
            there_v, there_c = there[:NV], there[NV:]
            put(n * step, outer_rows(own_c, there_c))
            put(n * step + PAIRS, outer_rows(there_v, own_v))
            put(n * step + 2 * PAIRS, outer_rows(there_v, there_c))
        put(NOFF * step, outer_rows(own_c, own_v))
        vec = vec_ref[pl.ds(pl.multiple_of(s * chunk, chunk), chunk), :]
        acc_ref[...] += jnp.dot(pts_ref[...], vec, preferred_element_type=jnp.float32)
        return carry

    acc_ref[...] = jnp.zeros_like(acc_ref)
    lax.fori_loop(0, parts, add_chunk, 0)
    own_x = acc_ref[NOFF * step :, :].astype(jnp.bfloat16).astype(jnp.float32)
    weighted = (own_x * bare_ref[...]).astype(jnp.bfloat16)
    for i in range(NOFF):
        start = (NOFF - 1 - i) * step
        cond_ref[i * PAIRS : (i + 1) * PAIRS, :] = acc_ref[start : start + PAIRS, :].astype(
            jnp.bfloat16
        )
        vale_ref[i * PAIRS : (i + 1) * PAIRS, :] = acc_ref[
            start + PAIRS : start + 2 * PAIRS, :
        ].astype(jnp.bfloat16)
        there_x = acc_ref[start + 2 * PAIRS : start + 3 * PAIRS, :].astype(jnp.bfloat16)
        term = lax.dot_general(
            weighted, there_x, (((1,), (1,)), ((), ())), preferred_element_type=jnp.float32
        )
        exch_ref[i * NV : (i + 1) * NV, :] = jnp.concatenate(
            [term[c * NV : (c + 1) * NV] for c in range(NC)], axis=1
        )
    source = lax.broadcasted_iota(jnp.int32, perm_ref.shape, 0)
    target = lax.broadcasted_iota(jnp.int32, perm_ref.shape, 1)
    moved = ((source >> 3) & 7) * (NV * NC) + (source >> 6) * NC + (source & 7)
    perm_ref[...] = jnp.where(moved == target, 1.0, 0.0).astype(jnp.bfloat16)


def waves_of(full, interp_vectors, bare):
    ng = interp_vectors.shape[1]
    total = NOFF * 3 * PAIRS + PAIRS
    flops = 2 * total * interp_vectors.shape[0] * ng
    columns = NC * NV * NC
    return pl.pallas_call(
        waves_kernel,
        out_shape=(
            jax.ShapeDtypeStruct((NOFF * PAIRS, ng), jnp.bfloat16),
            jax.ShapeDtypeStruct((NOFF * PAIRS, ng), jnp.bfloat16),
            jax.ShapeDtypeStruct((NOFF * NV, columns), jnp.float32),
            jax.ShapeDtypeStruct((columns, columns), jnp.bfloat16),
        ),
        in_specs=[VMEM] * 3,
        out_specs=(VMEM,) * 4,
        scratch_shapes=[
            pltpu.VMEM((total, full.shape[2]), jnp.bfloat16),
            pltpu.VMEM((total, ng), jnp.float32),
        ],
        cost_estimate=pl.CostEstimate(
            flops=flops, bytes_accessed=6 * 1024 * 1024, transcendentals=0
        ),
        compiler_params=pltpu.CompilerParams(vmem_limit_bytes=16 << 20),
        name="pair_waves",
    )(full, interp_vectors, bare)


def final_kernel(rows_ref, cond_ref, vale_ref, exch_ref, perm_ref, out_ref, all_ref, parts_ref):
    screen = rows_ref[0].astype(jnp.float32)
    for b in range(1, rows_ref.shape[0]):
        screen = screen + rows_ref[b].astype(jnp.float32)
    for i in range(NOFF):
        weighted = (
            cond_ref[i * PAIRS : (i + 1) * PAIRS, :].astype(jnp.float32) * screen[i : i + 1]
        ).astype(jnp.bfloat16)
        direct = lax.dot_general(
            vale_ref[i * PAIRS : (i + 1) * PAIRS, :],
            weighted,
            (((1,), (1,)), ((), ())),
            preferred_element_type=jnp.float32,
        )
        all_ref[i * NV : (i + 1) * NV, :] = jnp.concatenate(
            [direct[v * NV : (v + 1) * NV] for v in range(NV)], axis=1
        )
    value = all_ref[...]
    high = value.astype(jnp.bfloat16)
    rest = value - high.astype(jnp.float32)
    middle = rest.astype(jnp.bfloat16)
    low = (rest - middle.astype(jnp.float32)).astype(jnp.bfloat16)
    perm = perm_ref[...]
    moved = (
        jnp.dot(high, perm, preferred_element_type=jnp.float32)
        + jnp.dot(middle, perm, preferred_element_type=jnp.float32)
        + jnp.dot(low, perm, preferred_element_type=jnp.float32)
    )
    partial = 2.0 * exch_ref[...] - moved
    for p in range(parts_ref.shape[0]):
        lanes = slice(p * LANES, (p + 1) * LANES)
        parts_ref[p] = partial[:, lanes]
        for v in range(NV):
            out_ref[v, :, lanes] = parts_ref[p, pl.ds(v, NOFF, stride=NV), :]


def final_terms(rows, cond, vale, exch, perm):
    return pl.pallas_call(
        final_kernel,
        out_shape=jax.ShapeDtypeStruct((NV, NOFF, NC * NV * NC), jnp.float32),
        in_specs=[VMEM] * 5,
        out_specs=VMEM,
        scratch_shapes=[
            pltpu.VMEM((NOFF * NV, NC * NV * NC), jnp.float32),
            pltpu.VMEM((NC * NV * NC // LANES, NOFF * NV, LANES), jnp.float32),
        ],
        compiler_params=pltpu.CompilerParams(vmem_limit_bytes=6 << 20),
        name="final_terms",
    )(rows, cond, vale, exch, perm)


def per_device(orbitals, interp_vectors, screening, bare_coulomb, slab_kpoints):
    size = lax.axis_size("ka")
    parts = lax.axis_size("ga")
    blocks = size // NEAR
    place = lax.axis_index("ka").astype(jnp.int32).reshape(1)
    near = near_groups(size)
    far = far_groups(size)
    message = message_of(slab_kpoints, orbitals[0])
    block = swap(message, "ka", near)
    coords, edge = edges_of(place, block, blocks)
    grid = swap(coords, "ka", far)
    edge = lax.ppermute(edge, "ka", edge_route(size))
    window = window_of(place, block, edge, parts)
    full = swap(window, "ga")
    picked = pick_rows(place, grid.reshape(size, 2 * LANES), screening)
    arrived = swap(picked.reshape(NEAR, blocks * NOFF, -1), "ka", near)
    summed = near_sum(arrived, blocks)
    summed, full = lax.optimization_barrier((summed, full))
    rows = swap(summed, "ka", far)
    cond, vale, exch, perm = waves_of(full, interp_vectors, bare_coulomb[None])
    partial = final_terms(rows, cond, vale, exch, perm)
    terms = swap(partial, "ga")
    return result_of(terms)[None, :, None, :]


def solution(mesh):
    in_specs = (P("ka", None, "ga"), P(None, "ga"), P("ka", "ga"), P("ga"), P("ka"))
    out_specs = P("ka", None, None, "ga")
    return jax.shard_map(
        per_device, mesh=mesh, in_specs=in_specs, out_specs=out_specs, check_vma=False
    )
```

```python
import jax
import jax.numpy as jnp
from jax import lax
from jax.experimental import pallas as pl
from jax.experimental.pallas import tpu as pltpu
from jax.sharding import PartitionSpec as P


NV = 8
NC = 8
NG = 4096
NKX = 96
RSTEPS = 3
NOFF = 2 * RSTEPS + 1
NEAR = 8
LANES = 128
BANDS = NV + NC
PAIRS = NC * NC


def near_groups(size):
    return [[start + j for j in range(NEAR)] for start in range(0, size, NEAR)]


def far_groups(size):
    return [[j + start for start in range(0, size, NEAR)] for j in range(NEAR)]


def swap(tiles, axis, groups=None):
    return lax.all_to_all(tiles, axis, 0, 0, tiled=True, axis_index_groups=groups)


VMEM = pl.BlockSpec(memory_space=pltpu.VMEM)
SMEM = pl.BlockSpec(memory_space=pltpu.SMEM)


def message_kernel(point_ref, own_ref, out_ref):
    chunk = own_ref.shape[1]
    row = point_ref[0] // NKX
    col = point_ref[0] - row * NKX
    lane = lax.broadcasted_iota(jnp.int32, (NEAR, chunk), 1)
    coords = jnp.where(lane < LANES, row, col).astype(jnp.float32).astype(jnp.bfloat16)
    for j in range(out_ref.shape[0]):
        out_ref[j, :BANDS, :] = own_ref[...]
        out_ref[j, BANDS:, :] = coords


def message_of(points, own):
    return pl.pallas_call(
        message_kernel,
        out_shape=jax.ShapeDtypeStruct((NEAR, BANDS + NEAR, own.shape[1]), own.dtype),
        in_specs=[SMEM, VMEM],
        out_specs=VMEM,
        compiler_params=pltpu.CompilerParams(vmem_limit_bytes=2 << 20),
        name="message",
    )(points, own)


def edges_kernel(place_ref, block_ref, coords_ref, edge_ref):
    rows = [block_ref[j, BANDS : BANDS + 1, : 2 * LANES] for j in range(NEAR)]
    rows = jnp.concatenate([r.astype(jnp.float32) for r in rows], axis=0)
    for b in range(coords_ref.shape[0]):
        coords_ref[b] = rows.astype(jnp.bfloat16)
    inner = lax.rem(place_ref[0], NEAR)
    first = jnp.where(inner < NEAR // 2, 0, NEAR - RSTEPS)
    for n in range(RSTEPS):
        edge_ref[n * BANDS : (n + 1) * BANDS, :] = block_ref[first + n, :BANDS, :]


def edges_of(place, block, blocks):
    return pl.pallas_call(
        edges_kernel,
        out_shape=(
            jax.ShapeDtypeStruct((blocks, NEAR, 2 * LANES), block.dtype),
            jax.ShapeDtypeStruct((RSTEPS * BANDS, block.shape[2]), block.dtype),
        ),
        in_specs=[SMEM, VMEM],
        out_specs=(VMEM, VMEM),
        compiler_params=pltpu.CompilerParams(vmem_limit_bytes=2 << 20),
        name="edges",
    )(place, block)


def edge_route(size):
    route = []
    for k in range(size):
        start, inner = k - k % NEAR, k % NEAR
        if inner < RSTEPS:
            route.append((k, (start - NEAR + NEAR - 1 - inner) % size))
        elif inner >= NEAR - RSTEPS:
            route.append((k, (start + NEAR + NEAR - 1 - inner) % size))
    return route


def window_kernel(place_ref, block_ref, edge_ref, out_ref):
    inner = lax.rem(place_ref[0], NEAR)

    def put(n, value):
        out_ref[n * BANDS : (n + 1) * BANDS, :] = value

    for n in range(NOFF):
        at = inner + (n - RSTEPS)
        inside = jnp.logical_and(at >= 0, at < NEAR)
        over = jnp.where(at < 0, at + RSTEPS, at - NEAR)

        @pl.when(inside)
        def _():
            put(n, block_ref[at, :BANDS, :])

        @pl.when(jnp.logical_not(inside))
        def _():
            rows = pl.ds(pl.multiple_of(over * BANDS, BANDS), BANDS)
            put(n, edge_ref[rows, :])


def window_of(place, block, edge):
    return pl.pallas_call(
        window_kernel,
        out_shape=jax.ShapeDtypeStruct((NOFF * BANDS, block.shape[2]), block.dtype),
        in_specs=[SMEM, VMEM, VMEM],
        out_specs=VMEM,
        compiler_params=pltpu.CompilerParams(vmem_limit_bytes=4 << 20),
        name="window",
    )(place, block, edge)


def near_sum_kernel(rows_ref, out_ref):
    total = rows_ref[0].astype(jnp.float32)
    for b in range(1, rows_ref.shape[0]):
        total = total + rows_ref[b].astype(jnp.float32)
    for b in range(out_ref.shape[0]):
        out_ref[b] = total[b * NOFF : (b + 1) * NOFF].astype(out_ref.dtype)


def near_sum(rows, blocks):
    return pl.pallas_call(
        near_sum_kernel,
        out_shape=jax.ShapeDtypeStruct((blocks, NOFF, rows.shape[2]), rows.dtype),
        in_specs=[VMEM],
        out_specs=VMEM,
        compiler_params=pltpu.CompilerParams(vmem_limit_bytes=4 << 20),
        name="near_sum",
    )(rows)


def result_kernel(terms_ref, out_ref):
    total = terms_ref[0]
    for g in range(1, terms_ref.shape[0]):
        total = total + terms_ref[g]
    out_ref[...] = total * NG ** (-0.5)


def result_of(terms):
    return pl.pallas_call(
        result_kernel,
        out_shape=jax.ShapeDtypeStruct(terms.shape[1:], terms.dtype),
        in_specs=[VMEM],
        out_specs=VMEM,
        compiler_params=pltpu.CompilerParams(vmem_limit_bytes=2 << 20),
        name="result",
    )(terms)


def pick_kernel(place_ref, grid_ref, table_ref, out_ref, local_ref, hot_ref):
    size = grid_ref.shape[0]
    blocks = size // NEAR
    table_rows = table_ref.shape[0]
    row = grid_ref[:, :LANES].astype(jnp.float32)
    col = grid_ref[:, LANES:].astype(jnp.float32)
    base = (place_ref[0] * table_rows).astype(jnp.float32)
    for i in range(NOFF):
        d = i - RSTEPS
        row_step = row - jnp.roll(row, d, axis=0) if d else jnp.zeros_like(row)
        col_step = col - jnp.roll(col, d, axis=0) if d else jnp.zeros_like(col)
        row_step = jnp.where(row_step < 0, row_step + NKX, row_step)
        col_step = jnp.where(col_step < 0, col_step + NKX, col_step)
        local_ref[i * size : (i + 1) * size, :] = row_step * NKX + col_step - base
    lane = lax.broadcasted_iota(jnp.int32, (blocks, LANES), 1).astype(jnp.float32)
    for j in range(NEAR):
        for i in range(NOFF):
            local = local_ref[pl.ds(i * size + j, blocks, stride=NEAR), :]
            rows = pl.ds(j * blocks * NOFF + i, blocks, stride=NOFF)
            for part in range(hot_ref.shape[0]):
                hot_ref[part, rows, :] = jnp.where(local == lane + part * LANES, 1.0, 0.0)
    total = None
    for part in range(hot_ref.shape[0]):
        count = min(LANES, table_rows - part * LANES)
        term = jnp.dot(
            hot_ref[part, :, :count].astype(jnp.bfloat16),
            table_ref[part * LANES : part * LANES + count, :],
            preferred_element_type=jnp.float32,
        )
        total = term if total is None else total + term
    out_ref[...] = total.astype(jnp.bfloat16)


def pick_rows(place, grid, table):
    size = grid.shape[0]
    return pl.pallas_call(
        pick_kernel,
        out_shape=jax.ShapeDtypeStruct((size * NOFF, table.shape[1]), jnp.bfloat16),
        in_specs=[SMEM, VMEM, VMEM],
        out_specs=VMEM,
        scratch_shapes=[
            pltpu.VMEM((NOFF * size, LANES), jnp.float32),
            pltpu.VMEM((pl.cdiv(table.shape[0], LANES), size * NOFF, LANES), jnp.float32),
        ],
        compiler_params=pltpu.CompilerParams(vmem_limit_bytes=6 << 20),
        name="pick_rows",
    )(place, grid, table)


def outer_rows(singles, many):
    rows = []
    for h in range(0, singles.shape[0], 2):
        both = jnp.concatenate(
            [singles[h : h + 1] * many, singles[h + 1 : h + 2] * many], axis=0
        )
        rows.append(both.astype(jnp.bfloat16))
    return rows


GATHER_STEPS = (2, 1, 4)


def gather_mask(s):
    first, second, third = GATHER_STEPS
    return (s & 1) * first + ((s >> 1) & 1) * second + ((s >> 2) & 1) * third


def waves_kernel(
    part_ref,
    first_ref,
    second_ref,
    vec_ref,
    bare_ref,
    cond_ref,
    vale_ref,
    exch_ref,
    perm_ref,
    pts_ref,
    acc_ref,
):
    half = first_ref.shape[0]
    chunk = first_ref.shape[2]
    step = 3 * PAIRS

    def put(start, pieces):
        for h, piece in enumerate(pieces):
            pts_ref[start + 2 * NV * h : start + 2 * NV * (h + 1), :] = piece

    def add_chunk(source_ref, offset):
        def add(s, carry):
            own = source_ref[s, RSTEPS * BANDS : (RSTEPS + 1) * BANDS, :].astype(jnp.float32)
            own_v, own_c = own[:NV], own[NV:]
            for n in range(NOFF):
                there = source_ref[s, n * BANDS : (n + 1) * BANDS, :].astype(jnp.float32)
                there_v, there_c = there[:NV], there[NV:]
                put(n * step, outer_rows(own_c, there_c))
                put(n * step + PAIRS, outer_rows(there_v, own_v))
                put(n * step + 2 * PAIRS, outer_rows(there_v, there_c))
            put(NOFF * step, outer_rows(own_c, own_v))
            at = jnp.bitwise_xor(part_ref[0], gather_mask(s + offset))
            vec = vec_ref[pl.ds(pl.multiple_of(at * chunk, chunk), chunk), :]
            acc_ref[...] += jnp.dot(pts_ref[...], vec, preferred_element_type=jnp.float32)
            return carry

        return add

    acc_ref[...] = jnp.zeros_like(acc_ref)
    lax.fori_loop(0, half, add_chunk(first_ref, 0), 0)
    lax.fori_loop(0, half, add_chunk(second_ref, half), 0)
    own_x = acc_ref[NOFF * step :, :].astype(jnp.bfloat16).astype(jnp.float32)
    weighted = (own_x * bare_ref[...]).astype(jnp.bfloat16)
    for i in range(NOFF):
        start = (NOFF - 1 - i) * step
        cond_ref[i * PAIRS : (i + 1) * PAIRS, :] = acc_ref[start : start + PAIRS, :].astype(
            jnp.bfloat16
        )
        vale_ref[i * PAIRS : (i + 1) * PAIRS, :] = acc_ref[
            start + PAIRS : start + 2 * PAIRS, :
        ].astype(jnp.bfloat16)
        there_x = acc_ref[start + 2 * PAIRS : start + 3 * PAIRS, :].astype(jnp.bfloat16)
        term = lax.dot_general(
            weighted, there_x, (((1,), (1,)), ((), ())), preferred_element_type=jnp.float32
        )
        exch_ref[i * NV : (i + 1) * NV, :] = jnp.concatenate(
            [term[c * NV : (c + 1) * NV] for c in range(NC)], axis=1
        )
    source = lax.broadcasted_iota(jnp.int32, perm_ref.shape, 0)
    target = lax.broadcasted_iota(jnp.int32, perm_ref.shape, 1)
    moved = ((source >> 3) & 7) * (NV * NC) + (source >> 6) * NC + (source & 7)
    perm_ref[...] = jnp.where(moved == target, 1.0, 0.0).astype(jnp.bfloat16)


def waves_of(part, first, second, interp_vectors, bare):
    ng = interp_vectors.shape[1]
    total = NOFF * 3 * PAIRS + PAIRS
    flops = 2 * total * interp_vectors.shape[0] * ng
    columns = NC * NV * NC
    return pl.pallas_call(
        waves_kernel,
        out_shape=(
            jax.ShapeDtypeStruct((NOFF * PAIRS, ng), jnp.bfloat16),
            jax.ShapeDtypeStruct((NOFF * PAIRS, ng), jnp.bfloat16),
            jax.ShapeDtypeStruct((NOFF * NV, columns), jnp.float32),
            jax.ShapeDtypeStruct((columns, columns), jnp.bfloat16),
        ),
        in_specs=[SMEM] + [VMEM] * 4,
        out_specs=(VMEM,) * 4,
        scratch_shapes=[
            pltpu.VMEM((total, first.shape[2]), jnp.bfloat16),
            pltpu.VMEM((total, ng), jnp.float32),
        ],
        cost_estimate=pl.CostEstimate(
            flops=flops, bytes_accessed=6 * 1024 * 1024, transcendentals=0
        ),
        compiler_params=pltpu.CompilerParams(vmem_limit_bytes=16 << 20),
        name="pair_waves",
    )(part, first, second, interp_vectors, bare)


def final_kernel(rows_ref, cond_ref, vale_ref, exch_ref, perm_ref, out_ref, all_ref, parts_ref):
    screen = rows_ref[0].astype(jnp.float32)
    for b in range(1, rows_ref.shape[0]):
        screen = screen + rows_ref[b].astype(jnp.float32)
    for i in range(NOFF):
        weighted = (
            cond_ref[i * PAIRS : (i + 1) * PAIRS, :].astype(jnp.float32) * screen[i : i + 1]
        ).astype(jnp.bfloat16)
        direct = lax.dot_general(
            vale_ref[i * PAIRS : (i + 1) * PAIRS, :],
            weighted,
            (((1,), (1,)), ((), ())),
            preferred_element_type=jnp.float32,
        )
        all_ref[i * NV : (i + 1) * NV, :] = jnp.concatenate(
            [direct[v * NV : (v + 1) * NV] for v in range(NV)], axis=1
        )
    value = all_ref[...]
    high = value.astype(jnp.bfloat16)
    rest = value - high.astype(jnp.float32)
    middle = rest.astype(jnp.bfloat16)
    low = (rest - middle.astype(jnp.float32)).astype(jnp.bfloat16)
    perm = perm_ref[...]
    moved = (
        jnp.dot(high, perm, preferred_element_type=jnp.float32)
        + jnp.dot(middle, perm, preferred_element_type=jnp.float32)
        + jnp.dot(low, perm, preferred_element_type=jnp.float32)
    )
    partial = 2.0 * exch_ref[...] - moved
    for p in range(parts_ref.shape[0]):
        lanes = slice(p * LANES, (p + 1) * LANES)
        parts_ref[p] = partial[:, lanes]
        for v in range(NV):
            out_ref[v, :, lanes] = parts_ref[p, pl.ds(v, NOFF, stride=NV), :]


def final_terms(rows, cond, vale, exch, perm):
    return pl.pallas_call(
        final_kernel,
        out_shape=jax.ShapeDtypeStruct((NV, NOFF, NC * NV * NC), jnp.float32),
        in_specs=[VMEM] * 5,
        out_specs=VMEM,
        scratch_shapes=[
            pltpu.VMEM((NOFF * NV, NC * NV * NC), jnp.float32),
            pltpu.VMEM((NC * NV * NC // LANES, NOFF * NV, LANES), jnp.float32),
        ],
        compiler_params=pltpu.CompilerParams(vmem_limit_bytes=6 << 20),
        name="final_terms",
    )(rows, cond, vale, exch, perm)


def per_device(orbitals, interp_vectors, screening, bare_coulomb, slab_kpoints):
    size = lax.axis_size("ka")
    parts = lax.axis_size("ga")
    blocks = size // NEAR
    place = lax.axis_index("ka").astype(jnp.int32).reshape(1)
    part = lax.axis_index("ga").astype(jnp.int32).reshape(1)
    near = near_groups(size)
    far = far_groups(size)
    message = message_of(slab_kpoints, orbitals[0])
    block = swap(message, "ka", near)
    coords, edge = edges_of(place, block, blocks)
    grid = swap(coords, "ka", far)
    edge = lax.ppermute(edge, "ka", edge_route(size))
    window = window_of(place, block, edge)[None]
    swaps = [[(g, g ^ mask) for g in range(parts)] for mask in GATHER_STEPS]
    two = jnp.concatenate([window, lax.ppermute(window, "ga", swaps[0])])
    four = jnp.concatenate([two, lax.ppermute(two, "ga", swaps[1])])
    other = lax.ppermute(four, "ga", swaps[2])
    picked = pick_rows(place, grid.reshape(size, 2 * LANES), screening)
    arrived = swap(picked.reshape(NEAR, blocks * NOFF, -1), "ka", near)
    summed = near_sum(arrived, blocks)
    rows = swap(summed, "ka", far)
    cond, vale, exch, perm = waves_of(
        part, four, other, interp_vectors, bare_coulomb[None]
    )
    partial = final_terms(rows, cond, vale, exch, perm)
    terms = swap(partial, "ga")
    return result_of(terms)[None, :, None, :]


def solution(mesh):
    in_specs = (P("ka", None, "ga"), P(None, "ga"), P("ka", "ga"), P("ga"), P("ka"))
    out_specs = P("ka", None, None, "ga")
    return jax.shard_map(
        per_device, mesh=mesh, in_specs=in_specs, out_specs=out_specs, check_vma=False
    )
```

```python
import jax
import jax.numpy as jnp
from jax import lax
from jax.experimental import pallas as pl
from jax.experimental.pallas import tpu as pltpu
from jax.sharding import PartitionSpec as P


NV = 8
NC = 8
NG = 4096
NKX = 96
RSTEPS = 3
NOFF = 2 * RSTEPS + 1
NEAR = 8
LANES = 128
BANDS = NV + NC
PAIRS = NC * NC


def near_groups(size):
    return [[start + j for j in range(NEAR)] for start in range(0, size, NEAR)]


def far_groups(size):
    return [[j + start for start in range(0, size, NEAR)] for j in range(NEAR)]


def swap(tiles, axis, groups=None):
    return lax.all_to_all(tiles, axis, 0, 0, tiled=True, axis_index_groups=groups)


VMEM = pl.BlockSpec(memory_space=pltpu.VMEM)
SMEM = pl.BlockSpec(memory_space=pltpu.SMEM)


def message_kernel(point_ref, own_hbm, out_ref, own_ref, own_sem):
    own_copy = pltpu.make_async_copy(own_hbm, own_ref, own_sem)
    own_copy.start()
    chunk = own_ref.shape[1]
    row = point_ref[0] // NKX
    col = point_ref[0] - row * NKX
    lane = lax.broadcasted_iota(jnp.int32, (NEAR, chunk), 1)
    coords = jnp.where(lane < LANES, row, col).astype(jnp.float32).astype(jnp.bfloat16)
    for j in range(out_ref.shape[0]):
        out_ref[j, BANDS:, :] = coords
    own_copy.wait()
    for j in range(out_ref.shape[0]):
        out_ref[j, :BANDS, :] = own_ref[...]


def message_of(points, own):
    return pl.pallas_call(
        message_kernel,
        out_shape=jax.ShapeDtypeStruct((NEAR, BANDS + NEAR, own.shape[1]), own.dtype),
        in_specs=[SMEM, pl.BlockSpec(memory_space=pl.ANY)],
        out_specs=VMEM,
        scratch_shapes=[pltpu.VMEM(own.shape, own.dtype), pltpu.SemaphoreType.DMA],
        compiler_params=pltpu.CompilerParams(vmem_limit_bytes=67043328),
        name="message",
    )(points, own)


def edges_kernel(place_ref, block_ref, coords_ref, edge_ref):
    rows = [block_ref[j, BANDS : BANDS + 1, : 2 * LANES] for j in range(NEAR)]
    rows = jnp.concatenate([r.astype(jnp.float32) for r in rows], axis=0)
    for b in range(coords_ref.shape[0]):
        coords_ref[b] = rows.astype(jnp.bfloat16)
    inner = lax.rem(place_ref[0], NEAR)
    first = jnp.where(inner < NEAR // 2, 0, NEAR - RSTEPS)
    for n in range(RSTEPS):
        edge_ref[n * BANDS : (n + 1) * BANDS, :] = block_ref[first + n, :BANDS, :]


def edges_of(place, block, blocks):
    return pl.pallas_call(
        edges_kernel,
        out_shape=(
            jax.ShapeDtypeStruct((blocks, NEAR, 2 * LANES), block.dtype),
            jax.ShapeDtypeStruct((RSTEPS * BANDS, block.shape[2]), block.dtype),
        ),
        in_specs=[SMEM, VMEM],
        out_specs=(VMEM, VMEM),
        compiler_params=pltpu.CompilerParams(vmem_limit_bytes=2 << 20),
        name="edges",
    )(place, block)


def edge_route(size):
    route = []
    for k in range(size):
        start, inner = k - k % NEAR, k % NEAR
        if inner < RSTEPS:
            route.append((k, (start - NEAR + NEAR - 1 - inner) % size))
        elif inner >= NEAR - RSTEPS:
            route.append((k, (start + NEAR + NEAR - 1 - inner) % size))
    return route


def window_kernel(place_ref, block_ref, edge_ref, table_ref, out_ref, held_ref):
    held_ref[...] = table_ref[...]
    inner = lax.rem(place_ref[0], NEAR)

    def put(n, value):
        out_ref[n * BANDS : (n + 1) * BANDS, :] = value

    for n in range(NOFF):
        at = inner + (n - RSTEPS)
        inside = jnp.logical_and(at >= 0, at < NEAR)
        over = jnp.where(at < 0, at + RSTEPS, at - NEAR)

        @pl.when(inside)
        def _():
            put(n, block_ref[at, :BANDS, :])

        @pl.when(jnp.logical_not(inside))
        def _():
            rows = pl.ds(pl.multiple_of(over * BANDS, BANDS), BANDS)
            put(n, edge_ref[rows, :])


def window_of(place, block, edge, table):
    return pl.pallas_call(
        window_kernel,
        out_shape=(
            jax.ShapeDtypeStruct((NOFF * BANDS, block.shape[2]), block.dtype),
            jax.ShapeDtypeStruct(table.shape, table.dtype),
        ),
        in_specs=[SMEM, VMEM, VMEM, VMEM],
        out_specs=(VMEM, VMEM),
        compiler_params=pltpu.CompilerParams(vmem_limit_bytes=4 << 20),
        name="window",
    )(place, block, edge, table)


def near_sum_kernel(rows_ref, out_ref):
    total = rows_ref[0].astype(jnp.float32)
    for b in range(1, rows_ref.shape[0]):
        total = total + rows_ref[b].astype(jnp.float32)
    for b in range(out_ref.shape[0]):
        out_ref[b] = total[b * NOFF : (b + 1) * NOFF].astype(out_ref.dtype)


def near_sum(rows, blocks):
    return pl.pallas_call(
        near_sum_kernel,
        out_shape=jax.ShapeDtypeStruct((blocks, NOFF, rows.shape[2]), rows.dtype),
        in_specs=[VMEM],
        out_specs=VMEM,
        compiler_params=pltpu.CompilerParams(vmem_limit_bytes=4 << 20),
        name="near_sum",
    )(rows)


def result_kernel(terms_ref, out_ref):
    total = terms_ref[0]
    for g in range(1, terms_ref.shape[0]):
        total = total + terms_ref[g]
    out_ref[0, :, 0, :] = total * NG ** (-0.5)


def result_of(terms):
    return pl.pallas_call(
        result_kernel,
        out_shape=jax.ShapeDtypeStruct((1, NOFF, 1, terms.shape[2]), terms.dtype),
        in_specs=[VMEM],
        out_specs=VMEM,
        compiler_params=pltpu.CompilerParams(vmem_limit_bytes=2 << 20),
        name="result",
    )(terms)


def pick_kernel(place_ref, grid_ref, table_ref, out_ref, local_ref, hot_ref):
    size = grid_ref.shape[0]
    blocks = size // NEAR
    table_rows = table_ref.shape[0]
    row = grid_ref[:, :LANES].astype(jnp.float32)
    col = grid_ref[:, LANES:].astype(jnp.float32)
    base = (place_ref[0] * table_rows).astype(jnp.float32)
    for i in range(NOFF):
        d = i - RSTEPS
        row_step = row - jnp.roll(row, d, axis=0) if d else jnp.zeros_like(row)
        col_step = col - jnp.roll(col, d, axis=0) if d else jnp.zeros_like(col)
        row_step = jnp.where(row_step < 0, row_step + NKX, row_step)
        col_step = jnp.where(col_step < 0, col_step + NKX, col_step)
        local_ref[i * size : (i + 1) * size, :] = row_step * NKX + col_step - base
    lane = lax.broadcasted_iota(jnp.int32, (blocks, LANES), 1).astype(jnp.float32)
    for j in range(NEAR):
        for i in range(NOFF):
            local = local_ref[pl.ds(i * size + j, blocks, stride=NEAR), :]
            rows = pl.ds(j * blocks * NOFF + i, blocks, stride=NOFF)
            for part in range(hot_ref.shape[0]):
                hot_ref[part, rows, :] = jnp.where(local == lane + part * LANES, 1.0, 0.0)
    total = None
    for part in range(hot_ref.shape[0]):
        count = min(LANES, table_rows - part * LANES)
        term = jnp.dot(
            hot_ref[part, :, :count].astype(jnp.bfloat16),
            table_ref[part * LANES : part * LANES + count, :],
            preferred_element_type=jnp.float32,
        )
        total = term if total is None else total + term
    out_ref[...] = total.astype(jnp.bfloat16)


def pick_rows(place, grid, table):
    size = grid.shape[0]
    return pl.pallas_call(
        pick_kernel,
        out_shape=jax.ShapeDtypeStruct((size * NOFF, table.shape[1]), jnp.bfloat16),
        in_specs=[SMEM, VMEM, VMEM],
        out_specs=VMEM,
        scratch_shapes=[
            pltpu.VMEM((NOFF * size, LANES), jnp.float32),
            pltpu.VMEM((pl.cdiv(table.shape[0], LANES), size * NOFF, LANES), jnp.float32),
        ],
        compiler_params=pltpu.CompilerParams(vmem_limit_bytes=6 << 20),
        name="pick_rows",
    )(place, grid, table)


def outer_rows(singles, many):
    rows = []
    for h in range(0, singles.shape[0], 2):
        both = jnp.concatenate(
            [singles[h : h + 1] * many, singles[h + 1 : h + 2] * many], axis=0
        )
        rows.append(both.astype(jnp.bfloat16))
    return rows


GATHER_STEPS = (2, 1, 4)


def gather_mask(s):
    first, second, third = GATHER_STEPS
    return (s & 1) * first + ((s >> 1) & 1) * second + ((s >> 2) & 1) * third


def waves_kernel(
    part_ref,
    first_ref,
    second_ref,
    vec_hbm,
    bare_ref,
    cond_ref,
    vale_ref,
    exch_ref,
    perm_ref,
    all_ref,
    even_ref,
    odd_ref,
    acc_ref,
    vec_ref,
    vec_sem,
):
    half = first_ref.shape[0]
    chunk = first_ref.shape[2]
    step = 3 * PAIRS

    def vec_copy(s):
        at = jnp.bitwise_xor(part_ref[0], gather_mask(s)) * chunk
        source = vec_hbm.at[pl.ds(pl.multiple_of(at, chunk), chunk), :]
        return pltpu.make_async_copy(source, vec_ref.at[s], vec_sem.at[s])

    for s in range(2 * half):
        vec_copy(s).start()
    all_ref[:half] = first_ref[...]
    all_ref[half:] = second_ref[...]

    def build(s, pts_ref):
        def put(start, pieces):
            for h, piece in enumerate(pieces):
                pts_ref[start + 2 * NV * h : start + 2 * NV * (h + 1), :] = piece

        own = all_ref[s, RSTEPS * BANDS : (RSTEPS + 1) * BANDS, :].astype(jnp.float32)
        own_v, own_c = own[:NV], own[NV:]
        for n in range(NOFF):
            there = all_ref[s, n * BANDS : (n + 1) * BANDS, :].astype(jnp.float32)
            there_v, there_c = there[:NV], there[NV:]
            put(n * step, outer_rows(own_c, there_c))
            put(n * step + PAIRS, outer_rows(there_v, own_v))
            put(n * step + 2 * PAIRS, outer_rows(there_v, there_c))
        put(NOFF * step, outer_rows(own_c, own_v))

    def multiply(s, pts_ref):
        acc_ref[...] += jnp.dot(pts_ref[...], vec_ref[s], preferred_element_type=jnp.float32)

    build(0, even_ref)
    acc_ref[...] = jnp.zeros_like(acc_ref)

    def two_chunks(i, carry):
        s = 2 * i
        vec_copy(s).wait()
        build(s + 1, odd_ref)
        multiply(s, even_ref)
        vec_copy(s + 1).wait()
        build(jnp.minimum(s + 2, 2 * half - 1), even_ref)
        multiply(s + 1, odd_ref)
        return carry

    lax.fori_loop(0, half, two_chunks, 0)
    own_x = acc_ref[NOFF * step :, :].astype(jnp.bfloat16).astype(jnp.float32)
    weighted = (own_x * bare_ref[...]).astype(jnp.bfloat16)
    for i in range(NOFF):
        start = (NOFF - 1 - i) * step
        cond_ref[i * PAIRS : (i + 1) * PAIRS, :] = acc_ref[start : start + PAIRS, :].astype(
            jnp.bfloat16
        )
        vale_ref[i * PAIRS : (i + 1) * PAIRS, :] = acc_ref[
            start + PAIRS : start + 2 * PAIRS, :
        ].astype(jnp.bfloat16)
        there_x = acc_ref[start + 2 * PAIRS : start + 3 * PAIRS, :].astype(jnp.bfloat16)
        term = lax.dot_general(
            weighted, there_x, (((1,), (1,)), ((), ())), preferred_element_type=jnp.float32
        )
        exch_ref[i * NV : (i + 1) * NV, :] = jnp.concatenate(
            [term[c * NV : (c + 1) * NV] for c in range(NC)], axis=1
        )
    source = lax.broadcasted_iota(jnp.int32, perm_ref.shape, 0)
    target = lax.broadcasted_iota(jnp.int32, perm_ref.shape, 1)
    moved = ((source >> 3) & 7) * (NV * NC) + (source >> 6) * NC + (source & 7)
    perm_ref[...] = jnp.where(moved == target, 1.0, 0.0).astype(jnp.bfloat16)


def waves_of(part, first, second, interp_vectors, bare):
    ng = interp_vectors.shape[1]
    total = NOFF * 3 * PAIRS + PAIRS
    flops = 2 * total * interp_vectors.shape[0] * ng
    columns = NC * NV * NC
    return pl.pallas_call(
        waves_kernel,
        out_shape=(
            jax.ShapeDtypeStruct((NOFF * PAIRS, ng), jnp.bfloat16),
            jax.ShapeDtypeStruct((NOFF * PAIRS, ng), jnp.bfloat16),
            jax.ShapeDtypeStruct((NOFF * NV, columns), jnp.float32),
            jax.ShapeDtypeStruct((columns, columns), jnp.bfloat16),
        ),
        in_specs=[SMEM, VMEM, VMEM, pl.BlockSpec(memory_space=pl.ANY), VMEM],
        out_specs=(VMEM,) * 4,
        scratch_shapes=[
            pltpu.VMEM((2 * first.shape[0], *first.shape[1:]), jnp.bfloat16),
            pltpu.VMEM((total, first.shape[2]), jnp.bfloat16),
            pltpu.VMEM((total, first.shape[2]), jnp.bfloat16),
            pltpu.VMEM((total, ng), jnp.float32),
            pltpu.VMEM((2 * first.shape[0], first.shape[2], ng), jnp.bfloat16),
            pltpu.SemaphoreType.DMA((2 * first.shape[0],)),
        ],
        cost_estimate=pl.CostEstimate(
            flops=flops, bytes_accessed=6 * 1024 * 1024, transcendentals=0
        ),
        compiler_params=pltpu.CompilerParams(vmem_limit_bytes=50 << 20),
        name="pair_waves",
    )(part, first, second, interp_vectors, bare)


def final_kernel(rows_ref, cond_ref, vale_ref, exch_ref, perm_ref, out_ref, all_ref, parts_ref):
    screen = rows_ref[0].astype(jnp.float32)
    for b in range(1, rows_ref.shape[0]):
        screen = screen + rows_ref[b].astype(jnp.float32)
    for i in range(NOFF):
        weighted = (
            cond_ref[i * PAIRS : (i + 1) * PAIRS, :].astype(jnp.float32) * screen[i : i + 1]
        ).astype(jnp.bfloat16)
        direct = lax.dot_general(
            vale_ref[i * PAIRS : (i + 1) * PAIRS, :],
            weighted,
            (((1,), (1,)), ((), ())),
            preferred_element_type=jnp.float32,
        )
        all_ref[i * NV : (i + 1) * NV, :] = jnp.concatenate(
            [direct[v * NV : (v + 1) * NV] for v in range(NV)], axis=1
        )
    value = all_ref[...]
    high = value.astype(jnp.bfloat16)
    rest = value - high.astype(jnp.float32)
    middle = rest.astype(jnp.bfloat16)
    low = (rest - middle.astype(jnp.float32)).astype(jnp.bfloat16)
    perm = perm_ref[...]
    moved = (
        jnp.dot(high, perm, preferred_element_type=jnp.float32)
        + jnp.dot(middle, perm, preferred_element_type=jnp.float32)
        + jnp.dot(low, perm, preferred_element_type=jnp.float32)
    )
    partial = 2.0 * exch_ref[...] - moved
    for p in range(parts_ref.shape[0]):
        lanes = slice(p * LANES, (p + 1) * LANES)
        parts_ref[p] = partial[:, lanes]
        for v in range(NV):
            out_ref[v, :, lanes] = parts_ref[p, pl.ds(v, NOFF, stride=NV), :]


def final_terms(rows, cond, vale, exch, perm):
    return pl.pallas_call(
        final_kernel,
        out_shape=jax.ShapeDtypeStruct((NV, NOFF, NC * NV * NC), jnp.float32),
        in_specs=[VMEM] * 5,
        out_specs=VMEM,
        scratch_shapes=[
            pltpu.VMEM((NOFF * NV, NC * NV * NC), jnp.float32),
            pltpu.VMEM((NC * NV * NC // LANES, NOFF * NV, LANES), jnp.float32),
        ],
        compiler_params=pltpu.CompilerParams(vmem_limit_bytes=6 << 20),
        name="final_terms",
    )(rows, cond, vale, exch, perm)


def per_device(orbitals, interp_vectors, screening, bare_coulomb, slab_kpoints):
    size = lax.axis_size("ka")
    parts = lax.axis_size("ga")
    blocks = size // NEAR
    place = lax.axis_index("ka").astype(jnp.int32).reshape(1)
    part = lax.axis_index("ga").astype(jnp.int32).reshape(1)
    near = near_groups(size)
    far = far_groups(size)
    message = message_of(slab_kpoints, orbitals[0])
    block = swap(message, "ka", near)
    coords, edge = edges_of(place, block, blocks)
    grid = swap(coords, "ka", far)
    edge = lax.ppermute(edge, "ka", edge_route(size))
    window, table = window_of(place, block, edge, screening)
    window = window[None]
    swaps = [[(g, g ^ mask) for g in range(parts)] for mask in GATHER_STEPS]
    two = jnp.concatenate([window, lax.ppermute(window, "ga", swaps[0])])
    four = jnp.concatenate([two, lax.ppermute(two, "ga", swaps[1])])
    other = lax.ppermute(four, "ga", swaps[2])
    picked = pick_rows(place, grid.reshape(size, 2 * LANES), table)
    arrived = swap(picked.reshape(NEAR, blocks * NOFF, -1), "ka", near)
    summed = near_sum(arrived, blocks)
    rows = swap(summed, "ka", far)
    cond, vale, exch, perm = waves_of(
        part, four, other, interp_vectors, bare_coulomb[None]
    )
    partial = final_terms(rows, cond, vale, exch, perm)
    terms = swap(partial, "ga")
    return result_of(terms)


def solution(mesh):
    in_specs = (P("ka", None, "ga"), P(None, "ga"), P("ka", "ga"), P("ga"), P("ka"))
    out_specs = P("ka", None, None, "ga")
    return jax.shard_map(
        per_device, mesh=mesh, in_specs=in_specs, out_specs=out_specs, check_vma=False
    )
```

```python
import jax
import jax.numpy as jnp
from jax import lax
from jax.experimental import pallas as pl
from jax.experimental.pallas import tpu as pltpu
from jax.sharding import PartitionSpec as P


NV = 8
NC = 8
NG = 4096
NKX = 96
RSTEPS = 3
NOFF = 2 * RSTEPS + 1
NEAR = 8
LANES = 128
BANDS = NV + NC
PAIRS = NC * NC


def near_groups(size):
    return [[start + j for j in range(NEAR)] for start in range(0, size, NEAR)]


def far_groups(size, step):
    return [[j + start for start in range(0, size, step)] for j in range(step)]


def swap(tiles, axis, groups=None):
    return lax.all_to_all(tiles, axis, 0, 0, tiled=True, axis_index_groups=groups)


VMEM = pl.BlockSpec(memory_space=pltpu.VMEM)
SMEM = pl.BlockSpec(memory_space=pltpu.SMEM)


def message_kernel(point_ref, own_hbm, out_ref, own_ref, own_sem):
    own_copy = pltpu.make_async_copy(own_hbm, own_ref, own_sem)
    own_copy.start()
    chunk = own_ref.shape[1]
    row = point_ref[0] // NKX
    col = point_ref[0] - row * NKX
    lane = lax.broadcasted_iota(jnp.int32, (NEAR, chunk), 1)
    coords = jnp.where(lane < LANES, row, col).astype(jnp.float32).astype(jnp.bfloat16)
    for j in range(out_ref.shape[0]):
        out_ref[j, BANDS:, :] = coords
    own_copy.wait()
    for j in range(out_ref.shape[0]):
        out_ref[j, :BANDS, :] = own_ref[...]


def message_of(points, own):
    return pl.pallas_call(
        message_kernel,
        out_shape=jax.ShapeDtypeStruct((NEAR, BANDS + NEAR, own.shape[1]), own.dtype),
        in_specs=[SMEM, pl.BlockSpec(memory_space=pl.ANY)],
        out_specs=VMEM,
        scratch_shapes=[pltpu.VMEM(own.shape, own.dtype), pltpu.SemaphoreType.DMA],
        compiler_params=pltpu.CompilerParams(vmem_limit_bytes=67043328),
        name="message",
    )(points, own)


def edges_kernel(place_ref, block_ref, coords_ref, edge_ref):
    rows = [block_ref[j, BANDS : BANDS + 1, : 2 * LANES] for j in range(NEAR)]
    rows = jnp.concatenate([r.astype(jnp.float32) for r in rows], axis=0)
    for b in range(coords_ref.shape[0]):
        coords_ref[b] = rows.astype(jnp.bfloat16)
    inner = lax.rem(place_ref[0], NEAR)
    first = jnp.where(inner < NEAR // 2, 0, NEAR - RSTEPS)
    for n in range(RSTEPS):
        edge_ref[n * BANDS : (n + 1) * BANDS, :] = block_ref[first + n, :BANDS, :]


def edges_of(place, block, blocks):
    return pl.pallas_call(
        edges_kernel,
        out_shape=(
            jax.ShapeDtypeStruct((blocks, NEAR, 2 * LANES), block.dtype),
            jax.ShapeDtypeStruct((RSTEPS * BANDS, block.shape[2]), block.dtype),
        ),
        in_specs=[SMEM, VMEM],
        out_specs=(VMEM, VMEM),
        compiler_params=pltpu.CompilerParams(vmem_limit_bytes=2 << 20),
        name="edges",
    )(place, block)


def edge_route(size):
    route = []
    for k in range(size):
        start, inner = k - k % NEAR, k % NEAR
        if inner < RSTEPS:
            route.append((k, (start - NEAR + NEAR - 1 - inner) % size))
        elif inner >= NEAR - RSTEPS:
            route.append((k, (start + NEAR + NEAR - 1 - inner) % size))
    return route


def window_kernel(place_ref, block_ref, edge_ref, out_ref):
    inner = lax.rem(place_ref[0], NEAR)

    def put(n, value):
        out_ref[n * BANDS : (n + 1) * BANDS, :] = value

    for n in range(NOFF):
        at = inner + (n - RSTEPS)
        inside = jnp.logical_and(at >= 0, at < NEAR)
        over = jnp.where(at < 0, at + RSTEPS, at - NEAR)

        @pl.when(inside)
        def _():
            put(n, block_ref[at, :BANDS, :])

        @pl.when(jnp.logical_not(inside))
        def _():
            rows = pl.ds(pl.multiple_of(over * BANDS, BANDS), BANDS)
            put(n, edge_ref[rows, :])


def window_of(place, block, edge):
    return pl.pallas_call(
        window_kernel,
        out_shape=jax.ShapeDtypeStruct((NOFF * BANDS, block.shape[2]), block.dtype),
        in_specs=[SMEM, VMEM, VMEM],
        out_specs=VMEM,
        compiler_params=pltpu.CompilerParams(vmem_limit_bytes=4 << 20),
        name="window",
    )(place, block, edge)


def result_kernel(terms_ref, out_ref):
    total = terms_ref[0]
    for g in range(1, terms_ref.shape[0]):
        total = total + terms_ref[g]
    out_ref[0, :, 0, :] = total * NG ** (-0.5)


def result_of(terms):
    return pl.pallas_call(
        result_kernel,
        out_shape=jax.ShapeDtypeStruct((1, NOFF, 1, terms.shape[2]), terms.dtype),
        in_specs=[VMEM],
        out_specs=VMEM,
        compiler_params=pltpu.CompilerParams(vmem_limit_bytes=2 << 20),
        name="result",
    )(terms)


def table_mask(s):
    first, second = TABLE_STEPS
    return (s & 1) * first + ((s >> 1) & 1) * second


def pick_kernel(place_ref, grid_ref, table_ref, out_ref, column_ref, hot_ref):
    size = grid_ref.shape[0]
    pieces, table_rows, _ = table_ref.shape
    askers = size // pieces
    row = grid_ref[:, :LANES].astype(jnp.float32)
    col = grid_ref[:, LANES:].astype(jnp.float32)
    for i in range(NOFF):
        d = i - RSTEPS
        row_step = row - jnp.roll(row, d, axis=0) if d else jnp.zeros_like(row)
        col_step = col - jnp.roll(col, d, axis=0) if d else jnp.zeros_like(col)
        row_step = jnp.where(row_step < 0, row_step + NKX, row_step)
        col_step = jnp.where(col_step < 0, col_step + NKX, col_step)
        momentum = row_step * NKX + col_step
        column = jnp.full_like(momentum, -1.0)
        for s in range(pieces):
            base = (jnp.bitwise_xor(place_ref[0], table_mask(s)) * table_rows).astype(jnp.float32)
            local = momentum - base
            inside = jnp.logical_and(local >= 0, local < table_rows)
            column = jnp.where(inside, local + s * table_rows, column)
        column_ref[i * size : (i + 1) * size, :] = column
    lane = lax.broadcasted_iota(jnp.int32, (askers, LANES), 1).astype(jnp.float32)
    inner = lax.rem(place_ref[0], pieces)
    for i in range(NOFF):
        column = column_ref[pl.ds(i * size + inner, askers, stride=pieces), :]
        for part in range(hot_ref.shape[0]):
            hot_ref[part, pl.ds(i, askers, stride=NOFF), :] = jnp.where(
                column == lane + part * LANES, 1.0, 0.0
            )
    table = table_ref[...].reshape(pieces * table_rows, -1)
    total = None
    for part in range(hot_ref.shape[0]):
        count = min(LANES, table.shape[0] - part * LANES)
        term = jnp.dot(
            hot_ref[part, :, :count].astype(jnp.bfloat16),
            table[part * LANES : part * LANES + count, :],
            preferred_element_type=jnp.float32,
        )
        total = term if total is None else total + term
    for a in range(askers):
        out_ref[a] = total[a * NOFF : (a + 1) * NOFF].astype(jnp.bfloat16)


def pick_rows(place, grid, table):
    size = grid.shape[0]
    pieces, table_rows, width = table.shape
    askers = size // pieces
    return pl.pallas_call(
        pick_kernel,
        out_shape=jax.ShapeDtypeStruct((askers, NOFF, width), jnp.bfloat16),
        in_specs=[SMEM, VMEM, VMEM],
        out_specs=VMEM,
        scratch_shapes=[
            pltpu.VMEM((NOFF * size, LANES), jnp.float32),
            pltpu.VMEM(
                (pl.cdiv(pieces * table_rows, LANES), askers * NOFF, LANES), jnp.float32
            ),
        ],
        compiler_params=pltpu.CompilerParams(vmem_limit_bytes=6 << 20),
        name="pick_rows",
    )(place, grid, table)


def outer_rows(singles, many):
    rows = []
    for h in range(0, singles.shape[0], 2):
        both = jnp.concatenate(
            [singles[h : h + 1] * many, singles[h + 1 : h + 2] * many], axis=0
        )
        rows.append(both.astype(jnp.bfloat16))
    return rows


GATHER_STEPS = (4, 2, 1)
TABLE_STEPS = (1, 2)
FIRST_LIMIT = 50
SECOND_LIMIT = 47


def gather_mask(s):
    first, second, third = GATHER_STEPS
    return (s & 1) * first + ((s >> 1) & 1) * second + ((s >> 2) & 1) * third


def pair_products(
    part_ref, source_ref, vec_hbm, pts_ref, vec_ref, vec_sem, first
):
    count, _, chunk = source_ref.shape
    step = 3 * PAIRS

    def vec_copy(s):
        at = jnp.bitwise_xor(part_ref[0], gather_mask(first + s)) * chunk
        source = vec_hbm.at[pl.ds(pl.multiple_of(at, chunk), chunk), :]
        return pltpu.make_async_copy(
            source, vec_ref.at[s * chunk : (s + 1) * chunk, :], vec_sem.at[s]
        )

    for s in range(count):
        vec_copy(s).start()
    for s in range(count):

        def put(start, pieces):
            for h, piece in enumerate(pieces):
                rows = slice(start + 2 * NV * h, start + 2 * NV * (h + 1))
                pts_ref[rows, s * chunk : (s + 1) * chunk] = piece

        own = source_ref[s, RSTEPS * BANDS : (RSTEPS + 1) * BANDS, :].astype(jnp.float32)
        own_v, own_c = own[:NV], own[NV:]
        for n in range(NOFF):
            there = source_ref[s, n * BANDS : (n + 1) * BANDS, :].astype(jnp.float32)
            there_v, there_c = there[:NV], there[NV:]
            put(n * step, outer_rows(own_c, there_c))
            put(n * step + PAIRS, outer_rows(there_v, own_v))
            put(n * step + 2 * PAIRS, outer_rows(there_v, there_c))
        put(NOFF * step, outer_rows(own_c, own_v))
    for s in range(count):
        vec_copy(s).wait()
    return jnp.dot(pts_ref[...], vec_ref[...], preferred_element_type=jnp.float32)


def first_waves_kernel(part_ref, source_ref, vec_hbm, acc_ref, pts_ref, vec_ref, vec_sem):
    acc_ref[...] = pair_products(part_ref, source_ref, vec_hbm, pts_ref, vec_ref, vec_sem, 0)


def waves_kernel(
    part_ref,
    source_ref,
    vec_hbm,
    bare_ref,
    begun_ref,
    cond_ref,
    vale_ref,
    exch_ref,
    perm_ref,
    pts_ref,
    vec_ref,
    vec_sem,
    acc_ref,
):
    step = 3 * PAIRS
    acc_ref[...] = begun_ref[...] + pair_products(
        part_ref, source_ref, vec_hbm, pts_ref, vec_ref, vec_sem, source_ref.shape[0]
    )
    own_x = acc_ref[NOFF * step :, :].astype(jnp.bfloat16).astype(jnp.float32)
    weighted = (own_x * bare_ref[...]).astype(jnp.bfloat16)
    for i in range(NOFF):
        start = (NOFF - 1 - i) * step
        cond_ref[i * PAIRS : (i + 1) * PAIRS, :] = acc_ref[start : start + PAIRS, :].astype(
            jnp.bfloat16
        )
        vale_ref[i * PAIRS : (i + 1) * PAIRS, :] = acc_ref[
            start + PAIRS : start + 2 * PAIRS, :
        ].astype(jnp.bfloat16)
        there_x = acc_ref[start + 2 * PAIRS : start + 3 * PAIRS, :].astype(jnp.bfloat16)
        term = lax.dot_general(
            weighted, there_x, (((1,), (1,)), ((), ())), preferred_element_type=jnp.float32
        )
        exch_ref[i * NV : (i + 1) * NV, :] = jnp.concatenate(
            [term[c * NV : (c + 1) * NV] for c in range(NC)], axis=1
        )
    source = lax.broadcasted_iota(jnp.int32, perm_ref.shape, 0)
    target = lax.broadcasted_iota(jnp.int32, perm_ref.shape, 1)
    moved = ((source >> 3) & 7) * (NV * NC) + (source >> 6) * NC + (source & 7)
    perm_ref[...] = jnp.where(moved == target, 1.0, 0.0).astype(jnp.bfloat16)


def waves_scratch(source, ng):
    count, _, chunk = source.shape
    total = NOFF * 3 * PAIRS + PAIRS
    return [
        pltpu.VMEM((total, count * chunk), jnp.bfloat16),
        pltpu.VMEM((count * chunk, ng), jnp.bfloat16),
        pltpu.SemaphoreType.DMA((count,)),
    ]


def waves_cost(source, ng):
    total = NOFF * 3 * PAIRS + PAIRS
    flops = 2 * total * source.shape[0] * source.shape[2] * ng
    return pl.CostEstimate(flops=flops, bytes_accessed=6 * 1024 * 1024, transcendentals=0)


def first_waves_of(part, source, interp_vectors):
    ng = interp_vectors.shape[1]
    total = NOFF * 3 * PAIRS + PAIRS
    return pl.pallas_call(
        first_waves_kernel,
        out_shape=jax.ShapeDtypeStruct((total, ng), jnp.float32),
        in_specs=[SMEM, VMEM, pl.BlockSpec(memory_space=pl.ANY)],
        out_specs=VMEM,
        scratch_shapes=waves_scratch(source, ng),
        compiler_params=pltpu.CompilerParams(vmem_limit_bytes=FIRST_LIMIT << 20),
        cost_estimate=waves_cost(source, ng),
        name="first_waves",
    )(part, source, interp_vectors)


def waves_of(part, source, interp_vectors, bare, begun):
    ng = interp_vectors.shape[1]
    columns = NC * NV * NC
    return pl.pallas_call(
        waves_kernel,
        out_shape=(
            jax.ShapeDtypeStruct((NOFF * PAIRS, ng), jnp.bfloat16),
            jax.ShapeDtypeStruct((NOFF * PAIRS, ng), jnp.bfloat16),
            jax.ShapeDtypeStruct((NOFF * NV, columns), jnp.float32),
            jax.ShapeDtypeStruct((columns, columns), jnp.bfloat16),
        ),
        in_specs=[SMEM, VMEM, pl.BlockSpec(memory_space=pl.ANY), VMEM, VMEM],
        out_specs=(VMEM,) * 4,
        scratch_shapes=waves_scratch(source, ng) + [pltpu.VMEM(begun.shape, begun.dtype)],
        compiler_params=pltpu.CompilerParams(vmem_limit_bytes=SECOND_LIMIT << 20),
        cost_estimate=waves_cost(source, ng),
        name="pair_waves",
    )(part, source, interp_vectors, bare, begun)


def final_kernel(rows_ref, cond_ref, vale_ref, exch_ref, perm_ref, out_ref, all_ref, parts_ref):
    screen = rows_ref[0].astype(jnp.float32)
    for b in range(1, rows_ref.shape[0]):
        screen = screen + rows_ref[b].astype(jnp.float32)
    for i in range(NOFF):
        weighted = (
            cond_ref[i * PAIRS : (i + 1) * PAIRS, :].astype(jnp.float32) * screen[i : i + 1]
        ).astype(jnp.bfloat16)
        direct = lax.dot_general(
            vale_ref[i * PAIRS : (i + 1) * PAIRS, :],
            weighted,
            (((1,), (1,)), ((), ())),
            preferred_element_type=jnp.float32,
        )
        all_ref[i * NV : (i + 1) * NV, :] = jnp.concatenate(
            [direct[v * NV : (v + 1) * NV] for v in range(NV)], axis=1
        )
    value = all_ref[...]
    high = value.astype(jnp.bfloat16)
    rest = value - high.astype(jnp.float32)
    middle = rest.astype(jnp.bfloat16)
    low = (rest - middle.astype(jnp.float32)).astype(jnp.bfloat16)
    perm = perm_ref[...]
    moved = (
        jnp.dot(high, perm, preferred_element_type=jnp.float32)
        + jnp.dot(middle, perm, preferred_element_type=jnp.float32)
        + jnp.dot(low, perm, preferred_element_type=jnp.float32)
    )
    partial = 2.0 * exch_ref[...] - moved
    for p in range(parts_ref.shape[0]):
        lanes = slice(p * LANES, (p + 1) * LANES)
        parts_ref[p] = partial[:, lanes]
        for v in range(NV):
            out_ref[v, :, lanes] = parts_ref[p, pl.ds(v, NOFF, stride=NV), :]


def final_terms(rows, cond, vale, exch, perm):
    return pl.pallas_call(
        final_kernel,
        out_shape=jax.ShapeDtypeStruct((NV, NOFF, NC * NV * NC), jnp.float32),
        in_specs=[VMEM] * 5,
        out_specs=VMEM,
        scratch_shapes=[
            pltpu.VMEM((NOFF * NV, NC * NV * NC), jnp.float32),
            pltpu.VMEM((NC * NV * NC // LANES, NOFF * NV, LANES), jnp.float32),
        ],
        compiler_params=pltpu.CompilerParams(vmem_limit_bytes=6 << 20),
        name="final_terms",
    )(rows, cond, vale, exch, perm)


def per_device(orbitals, interp_vectors, screening, bare_coulomb, slab_kpoints):
    size = lax.axis_size("ka")
    parts = lax.axis_size("ga")
    blocks = size // NEAR
    place = lax.axis_index("ka").astype(jnp.int32).reshape(1)
    part = lax.axis_index("ga").astype(jnp.int32).reshape(1)
    near = near_groups(size)
    turns = [[(k, k ^ mask) for k in range(size)] for mask in TABLE_STEPS]
    swaps = [[(g, g ^ mask) for g in range(parts)] for mask in GATHER_STEPS]
    message = message_of(slab_kpoints, orbitals[0])
    block = swap(message, "ka", near)
    table = screening[None]
    table = jnp.concatenate([table, lax.ppermute(table, "ka", turns[0])])
    table = jnp.concatenate([table, lax.ppermute(table, "ka", turns[1])])
    coords, edge = edges_of(place, block, blocks)
    grid = swap(coords, "ka", far_groups(size, NEAR))
    edge = lax.ppermute(edge, "ka", edge_route(size))
    window = window_of(place, block, edge)[None]
    two = jnp.concatenate([window, lax.ppermute(window, "ga", swaps[0])])
    four = jnp.concatenate([two, lax.ppermute(two, "ga", swaps[1])])
    other = lax.ppermute(four, "ga", swaps[2])
    picked = pick_rows(place, grid.reshape(size, 2 * LANES), table)
    rows = swap(picked, "ka", far_groups(size, table.shape[0]))
    begun = first_waves_of(part, four, interp_vectors)
    cond, vale, exch, perm = waves_of(
        part, other, interp_vectors, bare_coulomb[None], begun
    )
    partial = final_terms(rows, cond, vale, exch, perm)
    terms = swap(partial, "ga")
    return result_of(terms)


def solution(mesh):
    in_specs = (P("ka", None, "ga"), P(None, "ga"), P("ka", "ga"), P("ga"), P("ka"))
    out_specs = P("ka", None, None, "ga")
    return jax.shard_map(
        per_device, mesh=mesh, in_specs=in_specs, out_specs=out_specs, check_vma=False
    )
```

```python
import jax
import jax.numpy as jnp
from jax import lax
from jax.experimental import pallas as pl
from jax.experimental.pallas import tpu as pltpu
from jax.sharding import PartitionSpec as P


NV = 8
NC = 8
NG = 4096
NKX = 96
RSTEPS = 3
NOFF = 2 * RSTEPS + 1
NEAR = 8
LANES = 128
BANDS = NV + NC
PAIRS = NC * NC


def near_groups(size):
    return [[start + j for j in range(NEAR)] for start in range(0, size, NEAR)]


def far_groups(size, step):
    return [[j + start for start in range(0, size, step)] for j in range(step)]


def swap(tiles, axis, groups=None):
    return lax.all_to_all(tiles, axis, 0, 0, tiled=True, axis_index_groups=groups)


VMEM = pl.BlockSpec(memory_space=pltpu.VMEM)
SMEM = pl.BlockSpec(memory_space=pltpu.SMEM)


def message_kernel(point_ref, own_hbm, out_ref, own_ref, own_sem):
    own_copy = pltpu.make_async_copy(own_hbm, own_ref, own_sem)
    own_copy.start()
    chunk = own_ref.shape[1]
    row = point_ref[0] // NKX
    col = point_ref[0] - row * NKX
    lane = lax.broadcasted_iota(jnp.int32, (NEAR, chunk), 1)
    coords = jnp.where(lane < LANES, row, col).astype(jnp.float32).astype(jnp.bfloat16)
    for j in range(out_ref.shape[0]):
        out_ref[j, BANDS:, :] = coords
    own_copy.wait()
    for j in range(out_ref.shape[0]):
        out_ref[j, :BANDS, :] = own_ref[...]


def message_of(points, own):
    return pl.pallas_call(
        message_kernel,
        out_shape=jax.ShapeDtypeStruct((NEAR, BANDS + NEAR, own.shape[1]), own.dtype),
        in_specs=[SMEM, pl.BlockSpec(memory_space=pl.ANY)],
        out_specs=VMEM,
        scratch_shapes=[pltpu.VMEM(own.shape, own.dtype), pltpu.SemaphoreType.DMA],
        compiler_params=pltpu.CompilerParams(vmem_limit_bytes=67043328),
        name="message",
    )(points, own)


def edges_kernel(place_ref, block_ref, coords_ref, edge_ref):
    rows = [block_ref[j, BANDS : BANDS + 1, : 2 * LANES] for j in range(NEAR)]
    rows = jnp.concatenate([r.astype(jnp.float32) for r in rows], axis=0)
    for b in range(coords_ref.shape[0]):
        coords_ref[b] = rows.astype(jnp.bfloat16)
    inner = lax.rem(place_ref[0], NEAR)
    first = jnp.where(inner < NEAR // 2, 0, NEAR - RSTEPS)
    for n in range(RSTEPS):
        edge_ref[n * BANDS : (n + 1) * BANDS, :] = block_ref[first + n, :BANDS, :]


def edges_of(place, block, blocks):
    return pl.pallas_call(
        edges_kernel,
        out_shape=(
            jax.ShapeDtypeStruct((blocks, NEAR, 2 * LANES), block.dtype),
            jax.ShapeDtypeStruct((RSTEPS * BANDS, block.shape[2]), block.dtype),
        ),
        in_specs=[SMEM, VMEM],
        out_specs=(VMEM, VMEM),
        compiler_params=pltpu.CompilerParams(vmem_limit_bytes=2 << 20),
        name="edges",
    )(place, block)


def edge_route(size):
    route = []
    for k in range(size):
        start, inner = k - k % NEAR, k % NEAR
        if inner < RSTEPS:
            route.append((k, (start - NEAR + NEAR - 1 - inner) % size))
        elif inner >= NEAR - RSTEPS:
            route.append((k, (start + NEAR + NEAR - 1 - inner) % size))
    return route


def window_kernel(place_ref, block_ref, edge_ref, out_ref):
    inner = lax.rem(place_ref[0], NEAR)

    def put(n, value):
        out_ref[n * BANDS : (n + 1) * BANDS, :] = value

    for n in range(NOFF):
        at = inner + (n - RSTEPS)
        inside = jnp.logical_and(at >= 0, at < NEAR)
        over = jnp.where(at < 0, at + RSTEPS, at - NEAR)

        @pl.when(inside)
        def _():
            put(n, block_ref[at, :BANDS, :])

        @pl.when(jnp.logical_not(inside))
        def _():
            rows = pl.ds(pl.multiple_of(over * BANDS, BANDS), BANDS)
            put(n, edge_ref[rows, :])


def window_of(place, block, edge):
    return pl.pallas_call(
        window_kernel,
        out_shape=jax.ShapeDtypeStruct((NOFF * BANDS, block.shape[2]), block.dtype),
        in_specs=[SMEM, VMEM, VMEM],
        out_specs=VMEM,
        compiler_params=pltpu.CompilerParams(vmem_limit_bytes=4 << 20),
        name="window",
    )(place, block, edge)


def result_kernel(terms_ref, out_ref):
    total = terms_ref[0]
    for g in range(1, terms_ref.shape[0]):
        total = total + terms_ref[g]
    out_ref[0, :, 0, :] = total * NG ** (-0.5)


def result_of(terms):
    return pl.pallas_call(
        result_kernel,
        out_shape=jax.ShapeDtypeStruct((1, NOFF, 1, terms.shape[2]), terms.dtype),
        in_specs=[VMEM],
        out_specs=VMEM,
        compiler_params=pltpu.CompilerParams(vmem_limit_bytes=2 << 20),
        name="result",
    )(terms)


def table_mask(s):
    first, second = TABLE_STEPS
    return (s & 1) * first + ((s >> 1) & 1) * second


def pick_kernel(place_ref, grid_ref, table_ref, other_ref, out_ref, column_ref, hot_ref):
    size = grid_ref.shape[0]
    half, table_rows, width = table_ref.shape
    pieces = 2 * half
    askers = size // pieces
    held = hot_ref.shape[0] // 2 * LANES
    row = grid_ref[:, :LANES].astype(jnp.float32)
    col = grid_ref[:, LANES:].astype(jnp.float32)
    for i in range(NOFF):
        d = i - RSTEPS
        row_step = row - jnp.roll(row, d, axis=0) if d else jnp.zeros_like(row)
        col_step = col - jnp.roll(col, d, axis=0) if d else jnp.zeros_like(col)
        row_step = jnp.where(row_step < 0, row_step + NKX, row_step)
        col_step = jnp.where(col_step < 0, col_step + NKX, col_step)
        momentum = row_step * NKX + col_step
        column = jnp.full_like(momentum, -1.0)
        for s in range(pieces):
            base = (jnp.bitwise_xor(place_ref[0], table_mask(s)) * table_rows).astype(jnp.float32)
            local = momentum - base
            inside = jnp.logical_and(local >= 0, local < table_rows)
            start = s // half * held + s % half * table_rows
            column = jnp.where(inside, local + start, column)
        column_ref[i * size : (i + 1) * size, :] = column
    lane = lax.broadcasted_iota(jnp.int32, (askers, LANES), 1).astype(jnp.float32)
    inner = lax.rem(place_ref[0], pieces)
    for i in range(NOFF):
        column = column_ref[pl.ds(i * size + inner, askers, stride=pieces), :]
        for part in range(hot_ref.shape[0]):
            hot_ref[part, pl.ds(i, askers, stride=NOFF), :] = jnp.where(
                column == lane + part * LANES, 1.0, 0.0
            )
    total = None
    for part in range(hot_ref.shape[0]):
        ref = table_ref if part * LANES < held else other_ref
        table = ref[...].reshape(half * table_rows, width)
        start = part * LANES % held
        count = min(LANES, half * table_rows - start)
        term = jnp.dot(
            hot_ref[part, :, :count].astype(jnp.bfloat16),
            table[start : start + count, :],
            preferred_element_type=jnp.float32,
        )
        total = term if total is None else total + term
    for a in range(askers):
        out_ref[a] = total[a * NOFF : (a + 1) * NOFF].astype(jnp.bfloat16)


def pick_rows(place, grid, table, other):
    size = grid.shape[0]
    half, table_rows, width = table.shape
    pieces = 2 * half
    askers = size // pieces
    return pl.pallas_call(
        pick_kernel,
        out_shape=jax.ShapeDtypeStruct((askers, NOFF, width), jnp.bfloat16),
        in_specs=[SMEM, VMEM, VMEM, VMEM],
        out_specs=VMEM,
        scratch_shapes=[
            pltpu.VMEM((NOFF * size, LANES), jnp.float32),
            pltpu.VMEM(
                (2 * pl.cdiv(half * table_rows, LANES), askers * NOFF, LANES), jnp.float32
            ),
        ],
        compiler_params=pltpu.CompilerParams(vmem_limit_bytes=6 << 20),
        name="pick_rows",
    )(place, grid, table, other)


def outer_rows(singles, many):
    rows = []
    for h in range(0, singles.shape[0], 2):
        both = jnp.concatenate(
            [singles[h : h + 1] * many, singles[h + 1 : h + 2] * many], axis=0
        )
        rows.append(both.astype(jnp.bfloat16))
    return rows


TABLE_STEPS = (1, 2)
FIRST_LIMIT = 50
SECOND_LIMIT = 47
RING = 4
OWN, FACING, NEXT, LAST = 0, 2, 1, 3
FIRST_PIECES = (OWN, FACING)
SECOND_PIECES = (NEXT, LAST)


def ring_route(parts, shift):
    return [
        (g // RING * RING + (g + shift) % RING, g) for g in range(parts)
    ]


def pair_products(part_ref, source_refs, vec_hbm, pts_ref, vec_ref, vec_sem, pieces):
    pair, _, chunk = source_refs[0].shape
    step = 3 * PAIRS

    def vec_copy(p, s):
        place = lax.rem(part_ref[0] + pieces[p], RING)
        line = jnp.bitwise_xor(part_ref[0] // RING, s)
        at = (line * RING + place) * chunk
        source = vec_hbm.at[pl.ds(pl.multiple_of(at, chunk), chunk), :]
        k = p * pair + s
        return pltpu.make_async_copy(
            source, vec_ref.at[k * chunk : (k + 1) * chunk, :], vec_sem.at[k]
        )

    every = [(p, s) for p in range(len(source_refs)) for s in range(pair)]
    for p, s in every:
        vec_copy(p, s).start()
    for p, s in every:
        lanes = slice((p * pair + s) * chunk, (p * pair + s + 1) * chunk)

        def put(start, values):
            for h, value in enumerate(values):
                pts_ref[start + 2 * NV * h : start + 2 * NV * (h + 1), lanes] = value

        source_ref = source_refs[p]
        own = source_ref[s, RSTEPS * BANDS : (RSTEPS + 1) * BANDS, :].astype(jnp.float32)
        own_v, own_c = own[:NV], own[NV:]
        for n in range(NOFF):
            there = source_ref[s, n * BANDS : (n + 1) * BANDS, :].astype(jnp.float32)
            there_v, there_c = there[:NV], there[NV:]
            put(n * step, outer_rows(own_c, there_c))
            put(n * step + PAIRS, outer_rows(there_v, own_v))
            put(n * step + 2 * PAIRS, outer_rows(there_v, there_c))
        put(NOFF * step, outer_rows(own_c, own_v))
    for p, s in every:
        vec_copy(p, s).wait()
    return jnp.dot(pts_ref[...], vec_ref[...], preferred_element_type=jnp.float32)


def first_waves_kernel(
    part_ref, one_ref, two_ref, vec_hbm, acc_ref, pts_ref, vec_ref, vec_sem
):
    acc_ref[...] = pair_products(
        part_ref, (one_ref, two_ref), vec_hbm, pts_ref, vec_ref, vec_sem, FIRST_PIECES
    )


def waves_kernel(
    part_ref,
    one_ref,
    two_ref,
    vec_hbm,
    bare_ref,
    begun_ref,
    cond_ref,
    vale_ref,
    exch_ref,
    perm_ref,
    pts_ref,
    vec_ref,
    vec_sem,
    acc_ref,
):
    step = 3 * PAIRS
    acc_ref[...] = begun_ref[...] + pair_products(
        part_ref, (one_ref, two_ref), vec_hbm, pts_ref, vec_ref, vec_sem, SECOND_PIECES
    )
    own_x = acc_ref[NOFF * step :, :].astype(jnp.bfloat16).astype(jnp.float32)
    weighted = (own_x * bare_ref[...]).astype(jnp.bfloat16)
    for i in range(NOFF):
        start = (NOFF - 1 - i) * step
        cond_ref[i * PAIRS : (i + 1) * PAIRS, :] = acc_ref[start : start + PAIRS, :].astype(
            jnp.bfloat16
        )
        vale_ref[i * PAIRS : (i + 1) * PAIRS, :] = acc_ref[
            start + PAIRS : start + 2 * PAIRS, :
        ].astype(jnp.bfloat16)
        there_x = acc_ref[start + 2 * PAIRS : start + 3 * PAIRS, :].astype(jnp.bfloat16)
        term = lax.dot_general(
            weighted, there_x, (((1,), (1,)), ((), ())), preferred_element_type=jnp.float32
        )
        exch_ref[i * NV : (i + 1) * NV, :] = jnp.concatenate(
            [term[c * NV : (c + 1) * NV] for c in range(NC)], axis=1
        )
    source = lax.broadcasted_iota(jnp.int32, perm_ref.shape, 0)
    target = lax.broadcasted_iota(jnp.int32, perm_ref.shape, 1)
    moved = ((source >> 3) & 7) * (NV * NC) + (source >> 6) * NC + (source & 7)
    perm_ref[...] = jnp.where(moved == target, 1.0, 0.0).astype(jnp.bfloat16)


def waves_scratch(source, ng):
    count, chunk = 2 * source.shape[0], source.shape[2]
    total = NOFF * 3 * PAIRS + PAIRS
    return [
        pltpu.VMEM((total, count * chunk), jnp.bfloat16),
        pltpu.VMEM((count * chunk, ng), jnp.bfloat16),
        pltpu.SemaphoreType.DMA((count,)),
    ]


def waves_cost(source, ng):
    total = NOFF * 3 * PAIRS + PAIRS
    flops = 4 * total * source.shape[0] * source.shape[2] * ng
    return pl.CostEstimate(flops=flops, bytes_accessed=6 * 1024 * 1024, transcendentals=0)


def first_waves_of(part, source, other, interp_vectors):
    ng = interp_vectors.shape[1]
    total = NOFF * 3 * PAIRS + PAIRS
    return pl.pallas_call(
        first_waves_kernel,
        out_shape=jax.ShapeDtypeStruct((total, ng), jnp.float32),
        in_specs=[SMEM, VMEM, VMEM, pl.BlockSpec(memory_space=pl.ANY)],
        out_specs=VMEM,
        scratch_shapes=waves_scratch(source, ng),
        compiler_params=pltpu.CompilerParams(vmem_limit_bytes=FIRST_LIMIT << 20),
        cost_estimate=waves_cost(source, ng),
        name="first_waves",
    )(part, source, other, interp_vectors)


def waves_of(part, source, other, interp_vectors, bare, begun):
    ng = interp_vectors.shape[1]
    columns = NC * NV * NC
    return pl.pallas_call(
        waves_kernel,
        out_shape=(
            jax.ShapeDtypeStruct((NOFF * PAIRS, ng), jnp.bfloat16),
            jax.ShapeDtypeStruct((NOFF * PAIRS, ng), jnp.bfloat16),
            jax.ShapeDtypeStruct((NOFF * NV, columns), jnp.float32),
            jax.ShapeDtypeStruct((columns, columns), jnp.bfloat16),
        ),
        in_specs=[SMEM, VMEM, VMEM, pl.BlockSpec(memory_space=pl.ANY), VMEM, VMEM],
        out_specs=(VMEM,) * 4,
        scratch_shapes=waves_scratch(source, ng) + [pltpu.VMEM(begun.shape, begun.dtype)],
        compiler_params=pltpu.CompilerParams(vmem_limit_bytes=SECOND_LIMIT << 20),
        cost_estimate=waves_cost(source, ng),
        name="pair_waves",
    )(part, source, other, interp_vectors, bare, begun)


def final_kernel(rows_ref, cond_ref, vale_ref, exch_ref, perm_ref, out_ref, all_ref, parts_ref):
    screen = rows_ref[0].astype(jnp.float32)
    for b in range(1, rows_ref.shape[0]):
        screen = screen + rows_ref[b].astype(jnp.float32)
    for i in range(NOFF):
        weighted = (
            cond_ref[i * PAIRS : (i + 1) * PAIRS, :].astype(jnp.float32) * screen[i : i + 1]
        ).astype(jnp.bfloat16)
        direct = lax.dot_general(
            vale_ref[i * PAIRS : (i + 1) * PAIRS, :],
            weighted,
            (((1,), (1,)), ((), ())),
            preferred_element_type=jnp.float32,
        )
        all_ref[i * NV : (i + 1) * NV, :] = jnp.concatenate(
            [direct[v * NV : (v + 1) * NV] for v in range(NV)], axis=1
        )
    value = all_ref[...]
    high = value.astype(jnp.bfloat16)
    rest = value - high.astype(jnp.float32)
    middle = rest.astype(jnp.bfloat16)
    low = (rest - middle.astype(jnp.float32)).astype(jnp.bfloat16)
    perm = perm_ref[...]
    moved = (
        jnp.dot(high, perm, preferred_element_type=jnp.float32)
        + jnp.dot(middle, perm, preferred_element_type=jnp.float32)
        + jnp.dot(low, perm, preferred_element_type=jnp.float32)
    )
    partial = 2.0 * exch_ref[...] - moved
    for p in range(parts_ref.shape[0]):
        lanes = slice(p * LANES, (p + 1) * LANES)
        parts_ref[p] = partial[:, lanes]
        for v in range(NV):
            out_ref[v, :, lanes] = parts_ref[p, pl.ds(v, NOFF, stride=NV), :]


def final_terms(rows, cond, vale, exch, perm):
    return pl.pallas_call(
        final_kernel,
        out_shape=jax.ShapeDtypeStruct((NV, NOFF, NC * NV * NC), jnp.float32),
        in_specs=[VMEM] * 5,
        out_specs=VMEM,
        scratch_shapes=[
            pltpu.VMEM((NOFF * NV, NC * NV * NC), jnp.float32),
            pltpu.VMEM((NC * NV * NC // LANES, NOFF * NV, LANES), jnp.float32),
        ],
        compiler_params=pltpu.CompilerParams(vmem_limit_bytes=6 << 20),
        name="final_terms",
    )(rows, cond, vale, exch, perm)


def per_device(orbitals, interp_vectors, screening, bare_coulomb, slab_kpoints):
    size = lax.axis_size("ka")
    parts = lax.axis_size("ga")
    blocks = size // NEAR
    place = lax.axis_index("ka").astype(jnp.int32).reshape(1)
    part = lax.axis_index("ga").astype(jnp.int32).reshape(1)
    near = near_groups(size)
    turns = [[(k, k ^ mask) for k in range(size)] for mask in TABLE_STEPS]
    across = [(g, g ^ RING) for g in range(parts)]
    message = message_of(slab_kpoints, orbitals[0])
    block = swap(message, "ka", near)
    table = screening[None]
    table = jnp.concatenate([table, lax.ppermute(table, "ka", turns[0])])
    other_table = lax.ppermute(table, "ka", turns[1])
    coords, edge = edges_of(place, block, blocks)
    grid = swap(coords, "ka", far_groups(size, NEAR))
    edge = lax.ppermute(edge, "ka", edge_route(size))
    window = window_of(place, block, edge)[None]
    two = jnp.concatenate([window, lax.ppermute(window, "ga", across)])
    facing = lax.ppermute(two, "ga", ring_route(parts, FACING))
    following = lax.ppermute(two, "ga", ring_route(parts, NEXT))
    previous = lax.ppermute(two, "ga", ring_route(parts, LAST))
    picked = pick_rows(place, grid.reshape(size, 2 * LANES), table, other_table)
    rows = swap(picked, "ka", far_groups(size, 2 * table.shape[0]))
    begun = first_waves_of(part, two, facing, interp_vectors)
    cond, vale, exch, perm = waves_of(
        part, following, previous, interp_vectors, bare_coulomb[None], begun
    )
    partial = final_terms(rows, cond, vale, exch, perm)
    terms = swap(partial, "ga")
    return result_of(terms)


def solution(mesh):
    in_specs = (P("ka", None, "ga"), P(None, "ga"), P("ka", "ga"), P("ga"), P("ka"))
    out_specs = P("ka", None, None, "ga")
    return jax.shard_map(
        per_device, mesh=mesh, in_specs=in_specs, out_specs=out_specs, check_vma=False
    )
```

```python
import jax
import jax.numpy as jnp
from jax import lax
from jax.experimental import pallas as pl
from jax.experimental.pallas import tpu as pltpu
from jax.sharding import PartitionSpec as P


NV = 8
NC = 8
NG = 4096
NKX = 96
RSTEPS = 3
NOFF = 2 * RSTEPS + 1
NEAR = 8
LANES = 128
BANDS = NV + NC
PAIRS = NC * NC


def near_groups(size):
    return [[start + j for j in range(NEAR)] for start in range(0, size, NEAR)]


def far_groups(size, step):
    return [[j + start for start in range(0, size, step)] for j in range(step)]


def swap(tiles, axis, groups=None):
    return lax.all_to_all(tiles, axis, 0, 0, tiled=True, axis_index_groups=groups)


VMEM = pl.BlockSpec(memory_space=pltpu.VMEM)
SMEM = pl.BlockSpec(memory_space=pltpu.SMEM)


def message_kernel(point_ref, own_hbm, out_ref, own_ref, own_sem):
    own_copy = pltpu.make_async_copy(own_hbm, own_ref, own_sem)
    own_copy.start()
    chunk = own_ref.shape[1]
    row = point_ref[0] // NKX
    col = point_ref[0] - row * NKX
    lane = lax.broadcasted_iota(jnp.int32, (NEAR, chunk), 1)
    coords = jnp.where(lane < LANES, row, col).astype(jnp.float32).astype(jnp.bfloat16)
    for j in range(out_ref.shape[0]):
        out_ref[j, BANDS:, :] = coords
    own_copy.wait()
    for j in range(out_ref.shape[0]):
        out_ref[j, :BANDS, :] = own_ref[...]


def message_of(points, own):
    return pl.pallas_call(
        message_kernel,
        out_shape=jax.ShapeDtypeStruct((NEAR, BANDS + NEAR, own.shape[1]), own.dtype),
        in_specs=[SMEM, pl.BlockSpec(memory_space=pl.ANY)],
        out_specs=VMEM,
        scratch_shapes=[pltpu.VMEM(own.shape, own.dtype), pltpu.SemaphoreType.DMA],
        compiler_params=pltpu.CompilerParams(vmem_limit_bytes=67043328),
        name="message",
    )(points, own)


def edges_kernel(place_ref, block_ref, coords_ref, edge_ref):
    rows = [block_ref[j, BANDS : BANDS + 1, : 2 * LANES] for j in range(NEAR)]
    rows = jnp.concatenate([r.astype(jnp.float32) for r in rows], axis=0)
    for b in range(coords_ref.shape[0]):
        coords_ref[b] = rows.astype(jnp.bfloat16)
    inner = lax.rem(place_ref[0], NEAR)
    first = jnp.where(inner < NEAR // 2, 0, NEAR - RSTEPS)
    for n in range(RSTEPS):
        edge_ref[n * BANDS : (n + 1) * BANDS, :] = block_ref[first + n, :BANDS, :]


def edges_of(place, block, blocks):
    return pl.pallas_call(
        edges_kernel,
        out_shape=(
            jax.ShapeDtypeStruct((blocks, NEAR, 2 * LANES), block.dtype),
            jax.ShapeDtypeStruct((RSTEPS * BANDS, block.shape[2]), block.dtype),
        ),
        in_specs=[SMEM, VMEM],
        out_specs=(VMEM, VMEM),
        compiler_params=pltpu.CompilerParams(vmem_limit_bytes=2 << 20),
        name="edges",
    )(place, block)


def edge_route(size):
    route = []
    for k in range(size):
        start, inner = k - k % NEAR, k % NEAR
        if inner < RSTEPS:
            route.append((k, (start - NEAR + NEAR - 1 - inner) % size))
        elif inner >= NEAR - RSTEPS:
            route.append((k, (start + NEAR + NEAR - 1 - inner) % size))
    return route


def window_kernel(place_ref, block_ref, edge_ref, out_ref):
    inner = lax.rem(place_ref[0], NEAR)

    def put(n, value):
        out_ref[n * BANDS : (n + 1) * BANDS, :] = value

    for n in range(NOFF):
        at = inner + (n - RSTEPS)
        inside = jnp.logical_and(at >= 0, at < NEAR)
        over = jnp.where(at < 0, at + RSTEPS, at - NEAR)

        @pl.when(inside)
        def _():
            put(n, block_ref[at, :BANDS, :])

        @pl.when(jnp.logical_not(inside))
        def _():
            rows = pl.ds(pl.multiple_of(over * BANDS, BANDS), BANDS)
            put(n, edge_ref[rows, :])


def window_of(place, block, edge):
    return pl.pallas_call(
        window_kernel,
        out_shape=jax.ShapeDtypeStruct((NOFF * BANDS, block.shape[2]), block.dtype),
        in_specs=[SMEM, VMEM, VMEM],
        out_specs=VMEM,
        compiler_params=pltpu.CompilerParams(vmem_limit_bytes=4 << 20),
        name="window",
    )(place, block, edge)


def result_kernel(terms_ref, out_ref):
    total = terms_ref[0]
    for g in range(1, terms_ref.shape[0]):
        total = total + terms_ref[g]
    out_ref[0, :, 0, :] = total * NG ** (-0.5)


def result_of(terms):
    return pl.pallas_call(
        result_kernel,
        out_shape=jax.ShapeDtypeStruct((1, NOFF, 1, terms.shape[2]), terms.dtype),
        in_specs=[VMEM],
        out_specs=VMEM,
        compiler_params=pltpu.CompilerParams(vmem_limit_bytes=2 << 20),
        name="result",
    )(terms)


def table_mask(s):
    first, second = TABLE_STEPS
    return (s & 1) * first + ((s >> 1) & 1) * second


def pick_kernel(place_ref, grid_ref, table_ref, other_ref, out_ref, column_ref, hot_ref):
    size = grid_ref.shape[0]
    half, table_rows, width = table_ref.shape
    pieces = 2 * half
    askers = size // pieces
    held = hot_ref.shape[0] // 2 * LANES
    row = grid_ref[:, :LANES].astype(jnp.float32)
    col = grid_ref[:, LANES:].astype(jnp.float32)
    for i in range(NOFF):
        d = i - RSTEPS
        row_step = row - jnp.roll(row, d, axis=0) if d else jnp.zeros_like(row)
        col_step = col - jnp.roll(col, d, axis=0) if d else jnp.zeros_like(col)
        row_step = jnp.where(row_step < 0, row_step + NKX, row_step)
        col_step = jnp.where(col_step < 0, col_step + NKX, col_step)
        momentum = row_step * NKX + col_step
        column = jnp.full_like(momentum, -1.0)
        for s in range(pieces):
            base = (jnp.bitwise_xor(place_ref[0], table_mask(s)) * table_rows).astype(jnp.float32)
            local = momentum - base
            inside = jnp.logical_and(local >= 0, local < table_rows)
            start = s // half * held + s % half * table_rows
            column = jnp.where(inside, local + start, column)
        column_ref[i * size : (i + 1) * size, :] = column
    lane = lax.broadcasted_iota(jnp.int32, (askers, LANES), 1).astype(jnp.float32)
    inner = lax.rem(place_ref[0], pieces)
    for i in range(NOFF):
        column = column_ref[pl.ds(i * size + inner, askers, stride=pieces), :]
        for part in range(hot_ref.shape[0]):
            hot_ref[part, pl.ds(i, askers, stride=NOFF), :] = jnp.where(
                column == lane + part * LANES, 1.0, 0.0
            )
    total = None
    for part in range(hot_ref.shape[0]):
        ref = table_ref if part * LANES < held else other_ref
        table = ref[...].reshape(half * table_rows, width)
        start = part * LANES % held
        count = min(LANES, half * table_rows - start)
        term = jnp.dot(
            hot_ref[part, :, :count].astype(jnp.bfloat16),
            table[start : start + count, :],
            preferred_element_type=jnp.float32,
        )
        total = term if total is None else total + term
    for a in range(askers):
        out_ref[a] = total[a * NOFF : (a + 1) * NOFF].astype(jnp.bfloat16)


def pick_rows(place, grid, table, other):
    size = grid.shape[0]
    half, table_rows, width = table.shape
    pieces = 2 * half
    askers = size // pieces
    return pl.pallas_call(
        pick_kernel,
        out_shape=jax.ShapeDtypeStruct((askers, NOFF, width), jnp.bfloat16),
        in_specs=[SMEM, VMEM, VMEM, VMEM],
        out_specs=VMEM,
        scratch_shapes=[
            pltpu.VMEM((NOFF * size, LANES), jnp.float32),
            pltpu.VMEM(
                (2 * pl.cdiv(half * table_rows, LANES), askers * NOFF, LANES), jnp.float32
            ),
        ],
        compiler_params=pltpu.CompilerParams(vmem_limit_bytes=6 << 20),
        name="pick_rows",
    )(place, grid, table, other)


def outer_rows(singles, many):
    rows = []
    for h in range(0, singles.shape[0], 2):
        both = jnp.concatenate(
            [singles[h : h + 1] * many, singles[h + 1 : h + 2] * many], axis=0
        )
        rows.append(both.astype(jnp.bfloat16))
    return rows


TABLE_STEPS = (1, 2)
FIRST_LIMIT = 48
SECOND_LIMIT = 20
RING = 4
OWN, FACING, NEXT, LAST = 0, 2, 1, 3
FIRST_PIECES = (OWN, FACING)
SECOND_PIECES = (NEXT, LAST)


def ring_route(parts, shift):
    return [
        (g // RING * RING + (g + shift) % RING, g) for g in range(parts)
    ]


def vec_copies(part_ref, vec_hbm, vec_ref, vec_sem, pieces):
    chunk = vec_ref.shape[1]
    copies = []
    for k in range(vec_ref.shape[0]):
        place = lax.rem(part_ref[0] + pieces[k // 2], RING)
        line = jnp.bitwise_xor(part_ref[0] // RING, k % 2)
        at = (line * RING + place) * chunk
        source = vec_hbm.at[pl.ds(pl.multiple_of(at, chunk), chunk), :]
        copies.append(pltpu.make_async_copy(source, vec_ref.at[k], vec_sem.at[k]))
    return copies


def pair_products(source_refs, pts_ref, vec_ref, copies=()):
    pair, _, chunk = source_refs[0].shape
    step = 3 * PAIRS
    every = [(p, s) for p in range(len(source_refs)) for s in range(pair)]
    for p, s in every:
        lanes = slice((p * pair + s) * chunk, (p * pair + s + 1) * chunk)

        def put(start, values):
            for h, value in enumerate(values):
                pts_ref[start + 2 * NV * h : start + 2 * NV * (h + 1), lanes] = value

        source_ref = source_refs[p]
        own = source_ref[s, RSTEPS * BANDS : (RSTEPS + 1) * BANDS, :].astype(jnp.float32)
        own_v, own_c = own[:NV], own[NV:]
        for n in range(NOFF):
            there = source_ref[s, n * BANDS : (n + 1) * BANDS, :].astype(jnp.float32)
            there_v, there_c = there[:NV], there[NV:]
            put(n * step, outer_rows(own_c, there_c))
            put(n * step + PAIRS, outer_rows(there_v, own_v))
            put(n * step + 2 * PAIRS, outer_rows(there_v, there_c))
    for copy in copies:
        copy.wait()
    vec = vec_ref[...].reshape(len(every) * chunk, -1)
    return jnp.dot(pts_ref[...], vec, preferred_element_type=jnp.float32)


def first_waves_kernel(
    part_ref, one_ref, two_ref, vec_hbm, acc_ref, next_ref, pts_ref, vec_ref, vec_sem, next_sem
):
    copies = vec_copies(part_ref, vec_hbm, vec_ref, vec_sem, FIRST_PIECES)
    later = vec_copies(part_ref, vec_hbm, next_ref, next_sem, SECOND_PIECES)
    for copy in copies + later:
        copy.start()
    acc_ref[...] = pair_products((one_ref, two_ref), pts_ref, vec_ref, copies)
    for copy in later:
        copy.wait()


def waves_kernel(
    one_ref,
    two_ref,
    vec_ref,
    bare_ref,
    begun_ref,
    cond_ref,
    vale_ref,
    exch_ref,
    perm_ref,
    pts_ref,
    acc_ref,
):
    step = 3 * PAIRS
    acc_ref[...] = begun_ref[...] + pair_products((one_ref, two_ref), pts_ref, vec_ref)
    own_start = RSTEPS * step + 2 * PAIRS
    own_x = acc_ref[own_start : own_start + PAIRS, :].astype(jnp.bfloat16)
    here = lax.broadcasted_iota(jnp.int32, (PAIRS, PAIRS), 0)
    there = lax.broadcasted_iota(jnp.int32, (PAIRS, PAIRS), 1)
    turned = (here & 7) * NC + (here >> 3) == there
    own_x = jnp.dot(
        jnp.where(turned, 1.0, 0.0).astype(jnp.bfloat16), own_x, preferred_element_type=jnp.float32
    )
    weighted = (own_x * bare_ref[...]).astype(jnp.bfloat16)
    for i in range(NOFF):
        start = (NOFF - 1 - i) * step
        cond_ref[i * PAIRS : (i + 1) * PAIRS, :] = acc_ref[start : start + PAIRS, :].astype(
            jnp.bfloat16
        )
        vale_ref[i * PAIRS : (i + 1) * PAIRS, :] = acc_ref[
            start + PAIRS : start + 2 * PAIRS, :
        ].astype(jnp.bfloat16)
        there_x = acc_ref[start + 2 * PAIRS : start + 3 * PAIRS, :].astype(jnp.bfloat16)
        term = lax.dot_general(
            weighted, there_x, (((1,), (1,)), ((), ())), preferred_element_type=jnp.float32
        )
        exch_ref[i * NV : (i + 1) * NV, :] = jnp.concatenate(
            [term[c * NV : (c + 1) * NV] for c in range(NC)], axis=1
        )
    source = lax.broadcasted_iota(jnp.int32, perm_ref.shape, 0)
    target = lax.broadcasted_iota(jnp.int32, perm_ref.shape, 1)
    moved = ((source >> 3) & 7) * (NV * NC) + (source >> 6) * NC + (source & 7)
    perm_ref[...] = jnp.where(moved == target, 1.0, 0.0).astype(jnp.bfloat16)


def waves_scratch(source):
    total = NOFF * 3 * PAIRS
    return [pltpu.VMEM((total, 2 * source.shape[0] * source.shape[2]), jnp.bfloat16)]


def waves_cost(source, ng):
    total = NOFF * 3 * PAIRS
    flops = 4 * total * source.shape[0] * source.shape[2] * ng
    return pl.CostEstimate(flops=flops, bytes_accessed=6 * 1024 * 1024, transcendentals=0)


def first_waves_of(part, source, other, interp_vectors):
    ng = interp_vectors.shape[1]
    total = NOFF * 3 * PAIRS
    count, chunk = 2 * source.shape[0], source.shape[2]
    return pl.pallas_call(
        first_waves_kernel,
        out_shape=(
            jax.ShapeDtypeStruct((total, ng), jnp.float32),
            jax.ShapeDtypeStruct((count, chunk, ng), interp_vectors.dtype),
        ),
        in_specs=[SMEM, VMEM, VMEM, pl.BlockSpec(memory_space=pl.ANY)],
        out_specs=(VMEM, VMEM),
        scratch_shapes=waves_scratch(source)
        + [
            pltpu.VMEM((count, chunk, ng), interp_vectors.dtype),
            pltpu.SemaphoreType.DMA((count,)),
            pltpu.SemaphoreType.DMA((count,)),
        ],
        compiler_params=pltpu.CompilerParams(vmem_limit_bytes=FIRST_LIMIT << 20),
        cost_estimate=waves_cost(source, ng),
        name="first_waves",
    )(part, source, other, interp_vectors)


def waves_of(source, other, vectors, bare, begun):
    ng = vectors.shape[2]
    columns = NC * NV * NC
    return pl.pallas_call(
        waves_kernel,
        out_shape=(
            jax.ShapeDtypeStruct((NOFF * PAIRS, ng), jnp.bfloat16),
            jax.ShapeDtypeStruct((NOFF * PAIRS, ng), jnp.bfloat16),
            jax.ShapeDtypeStruct((NOFF * NV, columns), jnp.float32),
            jax.ShapeDtypeStruct((columns, columns), jnp.bfloat16),
        ),
        in_specs=[VMEM] * 5,
        out_specs=(VMEM,) * 4,
        scratch_shapes=waves_scratch(source) + [pltpu.VMEM(begun.shape, begun.dtype)],
        compiler_params=pltpu.CompilerParams(vmem_limit_bytes=SECOND_LIMIT << 20),
        cost_estimate=waves_cost(source, ng),
        name="pair_waves",
    )(source, other, vectors, bare, begun)


def final_kernel(rows_ref, cond_ref, vale_ref, exch_ref, perm_ref, out_ref, all_ref, parts_ref):
    screen = rows_ref[0].astype(jnp.float32)
    for b in range(1, rows_ref.shape[0]):
        screen = screen + rows_ref[b].astype(jnp.float32)
    for i in range(NOFF):
        weighted = (
            cond_ref[i * PAIRS : (i + 1) * PAIRS, :].astype(jnp.float32) * screen[i : i + 1]
        ).astype(jnp.bfloat16)
        direct = lax.dot_general(
            vale_ref[i * PAIRS : (i + 1) * PAIRS, :],
            weighted,
            (((1,), (1,)), ((), ())),
            preferred_element_type=jnp.float32,
        )
        all_ref[i * NV : (i + 1) * NV, :] = jnp.concatenate(
            [direct[v * NV : (v + 1) * NV] for v in range(NV)], axis=1
        )
    value = all_ref[...]
    high = value.astype(jnp.bfloat16)
    rest = value - high.astype(jnp.float32)
    middle = rest.astype(jnp.bfloat16)
    low = (rest - middle.astype(jnp.float32)).astype(jnp.bfloat16)
    perm = perm_ref[...]
    moved = (
        jnp.dot(high, perm, preferred_element_type=jnp.float32)
        + jnp.dot(middle, perm, preferred_element_type=jnp.float32)
        + jnp.dot(low, perm, preferred_element_type=jnp.float32)
    )
    partial = 2.0 * exch_ref[...] - moved
    for p in range(parts_ref.shape[0]):
        lanes = slice(p * LANES, (p + 1) * LANES)
        parts_ref[p] = partial[:, lanes]
        for v in range(NV):
            out_ref[v, :, lanes] = parts_ref[p, pl.ds(v, NOFF, stride=NV), :]


def final_terms(rows, cond, vale, exch, perm):
    return pl.pallas_call(
        final_kernel,
        out_shape=jax.ShapeDtypeStruct((NV, NOFF, NC * NV * NC), jnp.float32),
        in_specs=[VMEM] * 5,
        out_specs=VMEM,
        scratch_shapes=[
            pltpu.VMEM((NOFF * NV, NC * NV * NC), jnp.float32),
            pltpu.VMEM((NC * NV * NC // LANES, NOFF * NV, LANES), jnp.float32),
        ],
        compiler_params=pltpu.CompilerParams(vmem_limit_bytes=6 << 20),
        name="final_terms",
    )(rows, cond, vale, exch, perm)


def per_device(orbitals, interp_vectors, screening, bare_coulomb, slab_kpoints):
    size = lax.axis_size("ka")
    parts = lax.axis_size("ga")
    blocks = size // NEAR
    place = lax.axis_index("ka").astype(jnp.int32).reshape(1)
    part = lax.axis_index("ga").astype(jnp.int32).reshape(1)
    near = near_groups(size)
    turns = [[(k, k ^ mask) for k in range(size)] for mask in TABLE_STEPS]
    across = [(g, g ^ RING) for g in range(parts)]
    message = message_of(slab_kpoints, orbitals[0])
    block = swap(message, "ka", near)
    table = screening[None]
    table = jnp.concatenate([table, lax.ppermute(table, "ka", turns[0])])
    other_table = lax.ppermute(table, "ka", turns[1])
    coords, edge = edges_of(place, block, blocks)
    grid = swap(coords, "ka", far_groups(size, NEAR))
    edge = lax.ppermute(edge, "ka", edge_route(size))
    window = window_of(place, block, edge)[None]
    two = jnp.concatenate([window, lax.ppermute(window, "ga", across)])
    facing = lax.ppermute(two, "ga", ring_route(parts, FACING))
    following = lax.ppermute(two, "ga", ring_route(parts, NEXT))
    previous = lax.ppermute(two, "ga", ring_route(parts, LAST))
    picked = pick_rows(place, grid.reshape(size, 2 * LANES), table, other_table)
    rows = swap(picked, "ka", far_groups(size, 2 * table.shape[0]))
    begun, vectors = first_waves_of(part, two, facing, interp_vectors)
    cond, vale, exch, perm = waves_of(
        following, previous, vectors, bare_coulomb[None], begun
    )
    partial = final_terms(rows, cond, vale, exch, perm)
    terms = swap(partial, "ga")
    return result_of(terms)


def solution(mesh):
    in_specs = (P("ka", None, "ga"), P(None, "ga"), P("ka", "ga"), P("ga"), P("ka"))
    out_specs = P("ka", None, None, "ga")
    return jax.shard_map(
        per_device, mesh=mesh, in_specs=in_specs, out_specs=out_specs, check_vma=False
    )
```

```python
import jax
import jax.numpy as jnp
from jax import lax
from jax.experimental import pallas as pl
from jax.experimental.pallas import tpu as pltpu
from jax.sharding import PartitionSpec as P


NV = 8
NC = 8
NG = 4096
NKX = 96
RSTEPS = 3
NOFF = 2 * RSTEPS + 1
NEAR = 8
LANES = 128
BANDS = NV + NC
PAIRS = NC * NC


def near_groups(size):
    return [[start + j for j in range(NEAR)] for start in range(0, size, NEAR)]


def far_groups(size, step):
    return [[j + start for start in range(0, size, step)] for j in range(step)]


def swap(tiles, axis, groups=None):
    return lax.all_to_all(tiles, axis, 0, 0, tiled=True, axis_index_groups=groups)


VMEM = pl.BlockSpec(memory_space=pltpu.VMEM)
SMEM = pl.BlockSpec(memory_space=pltpu.SMEM)


def message_kernel(point_ref, own_hbm, out_ref, own_ref, own_sem):
    own_copy = pltpu.make_async_copy(own_hbm, own_ref, own_sem)
    own_copy.start()
    chunk = own_ref.shape[1]
    row = point_ref[0] // NKX
    col = point_ref[0] - row * NKX
    lane = lax.broadcasted_iota(jnp.int32, (NEAR, chunk), 1)
    coords = jnp.where(lane < LANES, row, col).astype(jnp.float32).astype(jnp.bfloat16)
    for j in range(out_ref.shape[0]):
        out_ref[j, BANDS:, :] = coords
    own_copy.wait()
    for j in range(out_ref.shape[0]):
        out_ref[j, :BANDS, :] = own_ref[...]


def message_of(points, own):
    return pl.pallas_call(
        message_kernel,
        out_shape=jax.ShapeDtypeStruct((NEAR, BANDS + NEAR, own.shape[1]), own.dtype),
        in_specs=[SMEM, pl.BlockSpec(memory_space=pl.ANY)],
        out_specs=VMEM,
        scratch_shapes=[pltpu.VMEM(own.shape, own.dtype), pltpu.SemaphoreType.DMA],
        compiler_params=pltpu.CompilerParams(vmem_limit_bytes=67043328),
        name="message",
    )(points, own)


def edges_kernel(place_ref, block_ref, coords_ref, edge_ref):
    rows = [block_ref[j, BANDS : BANDS + 1, : 2 * LANES] for j in range(NEAR)]
    rows = jnp.concatenate([r.astype(jnp.float32) for r in rows], axis=0)
    for b in range(coords_ref.shape[0]):
        coords_ref[b] = rows.astype(jnp.bfloat16)
    inner = lax.rem(place_ref[0], NEAR)
    first = jnp.where(inner < NEAR // 2, 0, NEAR - RSTEPS)
    for n in range(RSTEPS):
        edge_ref[n * BANDS : (n + 1) * BANDS, :] = block_ref[first + n, :BANDS, :]


def edges_of(place, block, blocks):
    return pl.pallas_call(
        edges_kernel,
        out_shape=(
            jax.ShapeDtypeStruct((blocks, NEAR, 2 * LANES), block.dtype),
            jax.ShapeDtypeStruct((RSTEPS * BANDS, block.shape[2]), block.dtype),
        ),
        in_specs=[SMEM, VMEM],
        out_specs=(VMEM, VMEM),
        compiler_params=pltpu.CompilerParams(vmem_limit_bytes=2 << 20),
        name="edges",
    )(place, block)


def edge_route(size):
    route = []
    for k in range(size):
        start, inner = k - k % NEAR, k % NEAR
        if inner < RSTEPS:
            route.append((k, (start - NEAR + NEAR - 1 - inner) % size))
        elif inner >= NEAR - RSTEPS:
            route.append((k, (start + NEAR + NEAR - 1 - inner) % size))
    return route


def window_kernel(place_ref, block_ref, edge_ref, out_ref):
    inner = lax.rem(place_ref[0], NEAR)

    def put(n, value):
        out_ref[n * BANDS : (n + 1) * BANDS, :] = value

    for n in range(NOFF):
        at = inner + (n - RSTEPS)
        inside = jnp.logical_and(at >= 0, at < NEAR)
        over = jnp.where(at < 0, at + RSTEPS, at - NEAR)

        @pl.when(inside)
        def _():
            put(n, block_ref[at, :BANDS, :])

        @pl.when(jnp.logical_not(inside))
        def _():
            rows = pl.ds(pl.multiple_of(over * BANDS, BANDS), BANDS)
            put(n, edge_ref[rows, :])


def window_of(place, block, edge):
    return pl.pallas_call(
        window_kernel,
        out_shape=jax.ShapeDtypeStruct((NOFF * BANDS, block.shape[2]), block.dtype),
        in_specs=[SMEM, VMEM, VMEM],
        out_specs=VMEM,
        compiler_params=pltpu.CompilerParams(vmem_limit_bytes=4 << 20),
        name="window",
    )(place, block, edge)


def result_kernel(terms_ref, out_ref):
    total = terms_ref[0]
    for g in range(1, terms_ref.shape[0]):
        total = total + terms_ref[g]
    out_ref[0, :, 0, :] = total * NG ** (-0.5)


def result_of(terms):
    return pl.pallas_call(
        result_kernel,
        out_shape=jax.ShapeDtypeStruct((1, NOFF, 1, terms.shape[2]), terms.dtype),
        in_specs=[VMEM],
        out_specs=VMEM,
        compiler_params=pltpu.CompilerParams(vmem_limit_bytes=2 << 20),
        name="result",
    )(terms)


def table_mask(s):
    first, second = TABLE_STEPS
    return (s & 1) * first + ((s >> 1) & 1) * second


def pick_kernel(place_ref, grid_ref, table_ref, other_ref, out_ref, column_ref, hot_ref):
    size = grid_ref.shape[0]
    half, table_rows, width = table_ref.shape
    pieces = 2 * half
    askers = size // pieces
    held = hot_ref.shape[0] // 2 * LANES
    row = grid_ref[:, :LANES].astype(jnp.float32)
    col = grid_ref[:, LANES:].astype(jnp.float32)
    for i in range(NOFF):
        d = i - RSTEPS
        row_step = row - jnp.roll(row, d, axis=0) if d else jnp.zeros_like(row)
        col_step = col - jnp.roll(col, d, axis=0) if d else jnp.zeros_like(col)
        row_step = jnp.where(row_step < 0, row_step + NKX, row_step)
        col_step = jnp.where(col_step < 0, col_step + NKX, col_step)
        momentum = row_step * NKX + col_step
        column = jnp.full_like(momentum, -1.0)
        for s in range(pieces):
            base = (jnp.bitwise_xor(place_ref[0], table_mask(s)) * table_rows).astype(jnp.float32)
            local = momentum - base
            inside = jnp.logical_and(local >= 0, local < table_rows)
            start = s // half * held + s % half * table_rows
            column = jnp.where(inside, local + start, column)
        column_ref[i * size : (i + 1) * size, :] = column
    lane = lax.broadcasted_iota(jnp.int32, (askers, LANES), 1).astype(jnp.float32)
    inner = lax.rem(place_ref[0], pieces)
    for i in range(NOFF):
        column = column_ref[pl.ds(i * size + inner, askers, stride=pieces), :]
        for part in range(hot_ref.shape[0]):
            hot_ref[part, pl.ds(i, askers, stride=NOFF), :] = jnp.where(
                column == lane + part * LANES, 1.0, 0.0
            )
    total = None
    for part in range(hot_ref.shape[0]):
        ref = table_ref if part * LANES < held else other_ref
        table = ref[...].reshape(half * table_rows, width)
        start = part * LANES % held
        count = min(LANES, half * table_rows - start)
        term = jnp.dot(
            hot_ref[part, :, :count].astype(jnp.bfloat16),
            table[start : start + count, :],
            preferred_element_type=jnp.float32,
        )
        total = term if total is None else total + term
    for a in range(askers):
        out_ref[a] = total[a * NOFF : (a + 1) * NOFF].astype(jnp.bfloat16)


def pick_rows(place, grid, table, other):
    size = grid.shape[0]
    half, table_rows, width = table.shape
    pieces = 2 * half
    askers = size // pieces
    return pl.pallas_call(
        pick_kernel,
        out_shape=jax.ShapeDtypeStruct((askers, NOFF, width), jnp.bfloat16),
        in_specs=[SMEM, VMEM, VMEM, VMEM],
        out_specs=VMEM,
        scratch_shapes=[
            pltpu.VMEM((NOFF * size, LANES), jnp.float32),
            pltpu.VMEM(
                (2 * pl.cdiv(half * table_rows, LANES), askers * NOFF, LANES), jnp.float32
            ),
        ],
        compiler_params=pltpu.CompilerParams(vmem_limit_bytes=6 << 20),
        name="pick_rows",
    )(place, grid, table, other)


def outer_rows(singles, many):
    rows = []
    for h in range(0, singles.shape[0], 2):
        both = jnp.concatenate(
            [singles[h : h + 1] * many, singles[h + 1 : h + 2] * many], axis=0
        )
        rows.append(both.astype(jnp.bfloat16))
    return rows


TABLE_STEPS = (1, 2)
FIRST_LIMIT = 46
SECOND_LIMIT = 20
RING = 4
OWN, FACING, NEXT, LAST = 0, 2, 1, 3
FIRST_PIECES = (OWN, FACING)
SECOND_PIECES = (NEXT, LAST)


def ring_route(parts, shift):
    return [
        (g // RING * RING + (g + shift) % RING, g) for g in range(parts)
    ]


def vec_copies(part_ref, vec_hbm, vec_ref, vec_sem, pieces):
    chunk = vec_ref.shape[1]
    copies = []
    for k in range(vec_ref.shape[0]):
        place = lax.rem(part_ref[0] + pieces[k // 2], RING)
        line = jnp.bitwise_xor(part_ref[0] // RING, k % 2)
        at = (line * RING + place) * chunk
        source = vec_hbm.at[pl.ds(pl.multiple_of(at, chunk), chunk), :]
        copies.append(pltpu.make_async_copy(source, vec_ref.at[k], vec_sem.at[k]))
    return copies


def pair_products(source_refs, pts_ref, vec_ref, copies=(), later=()):
    pair, _, chunk = source_refs[0].shape
    step = 3 * PAIRS
    every = [(p, s) for p in range(len(source_refs)) for s in range(pair)]
    for p, s in every:
        lanes = slice((p * pair + s) * chunk, (p * pair + s + 1) * chunk)

        def put(start, values):
            for h, value in enumerate(values):
                pts_ref[start + 2 * NV * h : start + 2 * NV * (h + 1), lanes] = value

        source_ref = source_refs[p]
        own = source_ref[s, RSTEPS * BANDS : (RSTEPS + 1) * BANDS, :].astype(jnp.float32)
        own_v, own_c = own[:NV], own[NV:]
        for n in range(NOFF):
            there = source_ref[s, n * BANDS : (n + 1) * BANDS, :].astype(jnp.float32)
            there_v, there_c = there[:NV], there[NV:]
            put(n * step, outer_rows(own_c, there_c))
            put(n * step + PAIRS, outer_rows(there_v, own_v))
            put(n * step + 2 * PAIRS, outer_rows(there_v, there_c))
    for copy in copies:
        copy.wait()
    for copy in later:
        copy.start()
    vec = vec_ref[...].reshape(len(every) * chunk, -1)
    return jnp.dot(pts_ref[...], vec, preferred_element_type=jnp.float32)


def first_waves_kernel(
    part_ref, one_ref, two_ref, vec_hbm, acc_ref, next_ref, perm_ref, pts_ref, vec_ref,
    vec_sem, next_sem
):
    copies = vec_copies(part_ref, vec_hbm, vec_ref, vec_sem, FIRST_PIECES)
    later = vec_copies(part_ref, vec_hbm, next_ref, next_sem, SECOND_PIECES)
    for copy in copies:
        copy.start()
    acc_ref[...] = pair_products((one_ref, two_ref), pts_ref, vec_ref, copies, later)
    source = lax.broadcasted_iota(jnp.int32, perm_ref.shape, 0)
    target = lax.broadcasted_iota(jnp.int32, perm_ref.shape, 1)
    moved = ((source >> 3) & 7) * (NV * NC) + (source >> 6) * NC + (source & 7)
    perm_ref[...] = jnp.where(moved == target, 1.0, 0.0).astype(jnp.bfloat16)
    for copy in later:
        copy.wait()


def waves_kernel(
    one_ref,
    two_ref,
    vec_ref,
    bare_ref,
    begun_ref,
    cond_ref,
    vale_ref,
    exch_ref,
    pts_ref,
    acc_ref,
):
    step = 3 * PAIRS
    acc_ref[...] = begun_ref[...] + pair_products((one_ref, two_ref), pts_ref, vec_ref)
    own_start = RSTEPS * step + 2 * PAIRS
    own_x = acc_ref[own_start : own_start + PAIRS, :].astype(jnp.bfloat16)
    here = lax.broadcasted_iota(jnp.int32, (PAIRS, PAIRS), 0)
    there = lax.broadcasted_iota(jnp.int32, (PAIRS, PAIRS), 1)
    turned = (here & 7) * NC + (here >> 3) == there
    own_x = jnp.dot(
        jnp.where(turned, 1.0, 0.0).astype(jnp.bfloat16), own_x, preferred_element_type=jnp.float32
    )
    weighted = (own_x * bare_ref[...]).astype(jnp.bfloat16)
    for i in range(NOFF):
        start = (NOFF - 1 - i) * step
        cond_ref[i * PAIRS : (i + 1) * PAIRS, :] = acc_ref[start : start + PAIRS, :].astype(
            jnp.bfloat16
        )
        vale_ref[i * PAIRS : (i + 1) * PAIRS, :] = acc_ref[
            start + PAIRS : start + 2 * PAIRS, :
        ].astype(jnp.bfloat16)
        there_x = acc_ref[start + 2 * PAIRS : start + 3 * PAIRS, :].astype(jnp.bfloat16)
        term = lax.dot_general(
            weighted, there_x, (((1,), (1,)), ((), ())), preferred_element_type=jnp.float32
        )
        exch_ref[i * NV : (i + 1) * NV, :] = jnp.concatenate(
            [term[c * NV : (c + 1) * NV] for c in range(NC)], axis=1
        )


def waves_scratch(source):
    total = NOFF * 3 * PAIRS
    return [pltpu.VMEM((total, 2 * source.shape[0] * source.shape[2]), jnp.bfloat16)]


def waves_cost(source, ng):
    total = NOFF * 3 * PAIRS
    flops = 4 * total * source.shape[0] * source.shape[2] * ng
    return pl.CostEstimate(flops=flops, bytes_accessed=6 * 1024 * 1024, transcendentals=0)


def first_waves_of(part, source, other, interp_vectors):
    ng = interp_vectors.shape[1]
    total = NOFF * 3 * PAIRS
    count, chunk = 2 * source.shape[0], source.shape[2]
    columns = NC * NV * NC
    return pl.pallas_call(
        first_waves_kernel,
        out_shape=(
            jax.ShapeDtypeStruct((total, ng), jnp.float32),
            jax.ShapeDtypeStruct((count, chunk, ng), interp_vectors.dtype),
            jax.ShapeDtypeStruct((columns, columns), jnp.bfloat16),
        ),
        in_specs=[SMEM, VMEM, VMEM, pl.BlockSpec(memory_space=pl.ANY)],
        out_specs=(VMEM,) * 3,
        scratch_shapes=waves_scratch(source)
        + [
            pltpu.VMEM((count, chunk, ng), interp_vectors.dtype),
            pltpu.SemaphoreType.DMA((count,)),
            pltpu.SemaphoreType.DMA((count,)),
        ],
        compiler_params=pltpu.CompilerParams(vmem_limit_bytes=FIRST_LIMIT << 20),
        cost_estimate=waves_cost(source, ng),
        name="first_waves",
    )(part, source, other, interp_vectors)


def waves_of(source, other, vectors, bare, begun):
    ng = vectors.shape[2]
    columns = NC * NV * NC
    return pl.pallas_call(
        waves_kernel,
        out_shape=(
            jax.ShapeDtypeStruct((NOFF * PAIRS, ng), jnp.bfloat16),
            jax.ShapeDtypeStruct((NOFF * PAIRS, ng), jnp.bfloat16),
            jax.ShapeDtypeStruct((NOFF * NV, columns), jnp.float32),
        ),
        in_specs=[VMEM] * 5,
        out_specs=(VMEM,) * 3,
        scratch_shapes=waves_scratch(source) + [pltpu.VMEM(begun.shape, begun.dtype)],
        compiler_params=pltpu.CompilerParams(vmem_limit_bytes=SECOND_LIMIT << 20),
        cost_estimate=waves_cost(source, ng),
        name="pair_waves",
    )(source, other, vectors, bare, begun)


def final_kernel(rows_ref, cond_ref, vale_ref, exch_ref, perm_ref, out_ref, all_ref, parts_ref):
    screen = rows_ref[0].astype(jnp.float32)
    for b in range(1, rows_ref.shape[0]):
        screen = screen + rows_ref[b].astype(jnp.float32)
    for i in range(NOFF):
        weighted = (
            cond_ref[i * PAIRS : (i + 1) * PAIRS, :].astype(jnp.float32) * screen[i : i + 1]
        ).astype(jnp.bfloat16)
        direct = lax.dot_general(
            vale_ref[i * PAIRS : (i + 1) * PAIRS, :],
            weighted,
            (((1,), (1,)), ((), ())),
            preferred_element_type=jnp.float32,
        )
        all_ref[i * NV : (i + 1) * NV, :] = jnp.concatenate(
            [direct[v * NV : (v + 1) * NV] for v in range(NV)], axis=1
        )
    value = all_ref[...]
    high = value.astype(jnp.bfloat16)
    rest = value - high.astype(jnp.float32)
    middle = rest.astype(jnp.bfloat16)
    low = (rest - middle.astype(jnp.float32)).astype(jnp.bfloat16)
    perm = perm_ref[...]
    moved = (
        jnp.dot(high, perm, preferred_element_type=jnp.float32)
        + jnp.dot(middle, perm, preferred_element_type=jnp.float32)
        + jnp.dot(low, perm, preferred_element_type=jnp.float32)
    )
    partial = 2.0 * exch_ref[...] - moved
    for p in range(parts_ref.shape[0]):
        lanes = slice(p * LANES, (p + 1) * LANES)
        parts_ref[p] = partial[:, lanes]
        for v in range(NV):
            out_ref[v, :, lanes] = parts_ref[p, pl.ds(v, NOFF, stride=NV), :]


def final_terms(rows, cond, vale, exch, perm):
    return pl.pallas_call(
        final_kernel,
        out_shape=jax.ShapeDtypeStruct((NV, NOFF, NC * NV * NC), jnp.float32),
        in_specs=[VMEM] * 5,
        out_specs=VMEM,
        scratch_shapes=[
            pltpu.VMEM((NOFF * NV, NC * NV * NC), jnp.float32),
            pltpu.VMEM((NC * NV * NC // LANES, NOFF * NV, LANES), jnp.float32),
        ],
        compiler_params=pltpu.CompilerParams(vmem_limit_bytes=6 << 20),
        name="final_terms",
    )(rows, cond, vale, exch, perm)


def per_device(orbitals, interp_vectors, screening, bare_coulomb, slab_kpoints):
    size = lax.axis_size("ka")
    parts = lax.axis_size("ga")
    blocks = size // NEAR
    place = lax.axis_index("ka").astype(jnp.int32).reshape(1)
    part = lax.axis_index("ga").astype(jnp.int32).reshape(1)
    near = near_groups(size)
    turns = [[(k, k ^ mask) for k in range(size)] for mask in TABLE_STEPS]
    across = [(g, g ^ RING) for g in range(parts)]
    message = message_of(slab_kpoints, orbitals[0])
    block = swap(message, "ka", near)
    table = screening[None]
    table = jnp.concatenate([table, lax.ppermute(table, "ka", turns[0])])
    other_table = lax.ppermute(table, "ka", turns[1])
    coords, edge = edges_of(place, block, blocks)
    grid = swap(coords, "ka", far_groups(size, NEAR))
    edge = lax.ppermute(edge, "ka", edge_route(size))
    window = window_of(place, block, edge)[None]
    two = jnp.concatenate([window, lax.ppermute(window, "ga", across)])
    facing = lax.ppermute(two, "ga", ring_route(parts, FACING))
    following = lax.ppermute(two, "ga", ring_route(parts, NEXT))
    previous = lax.ppermute(two, "ga", ring_route(parts, LAST))
    picked = pick_rows(place, grid.reshape(size, 2 * LANES), table, other_table)
    rows = swap(picked, "ka", far_groups(size, 2 * table.shape[0]))
    begun, vectors, perm = first_waves_of(part, two, facing, interp_vectors)
    cond, vale, exch = waves_of(
        following, previous, vectors, bare_coulomb[None], begun
    )
    partial = final_terms(rows, cond, vale, exch, perm)
    terms = swap(partial, "ga")
    return result_of(terms)


def solution(mesh):
    in_specs = (P("ka", None, "ga"), P(None, "ga"), P("ka", "ga"), P("ga"), P("ka"))
    out_specs = P("ka", None, None, "ga")
    return jax.shard_map(
        per_device, mesh=mesh, in_specs=in_specs, out_specs=out_specs, check_vma=False
    )
```
